32 devices in a mesh: pool: 4 (over y, x), tp: 8 (over z, core).
Axes of the slice: x: 2, y: 2, z: 4, core: 2. Of those that a mesh axis runs over, the one named last changes fastest.
Arguments:
- prompt_states: bfloat16 [896, 8192], P(('pool', 'tp')), may hold values from -32 to 32
- stretch_slot: int32 [896], replicated, may hold values from 0 to 63, as said below
- cache_length: int32 [64], P(('pool', 'tp')), may hold values from 0 to 512, as said below
- cache_keys: bfloat16 [64, 512, 1024], P(('pool', 'tp')), may hold values from -64 to 64
- cache_values: bfloat16 [64, 512, 1024], P(('pool', 'tp')), may hold values from -6 to 6
- step_states: bfloat16 [4, 64, 8192], P(None, ('pool', 'tp')), may hold values from -6 to 6
- query_weight: bfloat16 [8192, 8192], P(None, 'tp'), may hold values from -0.0625 to 0.0625
- key_weight: bfloat16 [8192, 1024], P(None, 'tp'), may hold values from -0.0625 to 0.0625
- value_weight: bfloat16 [8192, 1024], P(None, 'tp'), may hold values from -0.0625 to 0.0625
Outputs:
- prompt_out: bfloat16 [896, 8192], P('pool', 'tp')
- step_out: bfloat16 [4, 64, 8192], P(None, ('pool', 'tp'))
The draws below stay inside these ranges and needn't reach their ends.
Inputs may be any that keep to these rules, and one draw needn't show every extreme that they name: `stretch_slot`: each group's 224 tokens are whole prompts of 24 to 32 tokens in consecutive runs; no slot is named by two prompts; some prompt has 32 tokens. `cache_length`: 0 for every slot that stretch_slot names, 1 or more for the others; some slot has 512.
All inputs are finite; a program needn't handle non-finite values.
Results may differ from the reference program's by a relative error of at most 0.0094.
Values may be sent and summed in bfloat16 or wider, within the bound.
A program may use at most 128 MiB of HBM per device.

```python
import math
import jax
import jax.numpy as jnp
from jax import lax

D = 8192
HEADS = 64
KV_HEADS = 8
HEAD = 128
PMAX = 32
CL = 512
STEPS = 4
PT = 224
R = 64
N_POOL = 4


def prompt_sizes(key):
    prompt_count = PT // (7 * PMAX // 8)
    lowest = 3 * PMAX // 4
    key_walk, key_group, key_index, key_donor = jax.random.split(key, 4)
    groups = jnp.arange(N_POOL, dtype=jnp.int32)
    places = jnp.arange(prompt_count, dtype=jnp.int32)
    sizing = jnp.full((N_POOL, prompt_count), 7 * PMAX // 8, jnp.int32)

    def wander(turn_index, current):
        endpoints = jax.random.randint(jax.random.fold_in(key_walk, turn_index), (2, N_POOL), 0, prompt_count)
        source = endpoints[0]
        target = endpoints[1]
        movable = (source != target) & (current[groups, source] > lowest) & (current[groups, target] < PMAX)
        amount = movable.astype(jnp.int32)
        current = current.at[groups, source].add(-amount)
        return current.at[groups, target].add(amount)
    sizing = lax.fori_loop(0, 16 * prompt_count, wander, sizing)
    chosen_group = jax.random.randint(key_group, (), 0, N_POOL)
    chosen = jax.random.randint(key_index, (), 0, prompt_count)

    def raise_chosen(turn_index, current):
        scores = jax.random.permutation(jax.random.fold_in(key_donor, turn_index), prompt_count).astype(jnp.int32)
        group_row = current[chosen_group]
        eligible = (places != chosen) & (group_row > lowest)
        donor_index = jnp.argmax(jnp.where(eligible, scores, -1))
        amount = (group_row[chosen] < PMAX).astype(jnp.int32)
        group_row = group_row.at[donor_index].add(-amount).at[chosen].add(amount)
        return current.at[chosen_group].set(group_row)
    return lax.fori_loop(0, PMAX - lowest, raise_chosen, sizing)


def arrange(key):
    drawn = jax.random.fold_in(key, 7)
    key_sizes, key_order, key_left, key_right = jax.random.split(drawn, 4)
    sizing = prompt_sizes(key_sizes)
    prompt_count = sizing.shape[1]
    ordering = jax.random.permutation(key_order, R)
    newcomers = N_POOL * prompt_count
    owners = ordering[:newcomers].reshape(N_POOL, prompt_count)
    endings = jnp.cumsum(sizing, axis=1)
    places = jnp.arange(PT)
    which_prompt = jnp.sum(places[None, :, None] >= endings[:, None, :], axis=2)
    stretch_slot = jnp.take_along_axis(owners, which_prompt, axis=1).reshape(N_POOL * PT)
    left_draw = jax.random.randint(key_left, (R,), 0, CL + 1)
    right_draw = jax.random.randint(key_right, (R,), 0, CL + 1)
    lengths = jnp.minimum(1 + left_draw * right_draw // CL, CL)
    lengths = lengths.at[owners.reshape(-1)].set(0)
    lengths = lengths.at[ordering[newcomers]].set(CL)
    return (stretch_slot.astype(jnp.int32), lengths.astype(jnp.int32))


def draw_stretch_slot(key, part):
    return arrange(key)[0]


def draw_cache_length(key, part):
    return arrange(key)[1]


def draw_prompt_states(key, part):
    shape = (N_POOL * PT, D)
    drawn = jax.random.normal(key, shape, jnp.float32)
    return jnp.clip(drawn, -32.0, 32.0).astype(jnp.bfloat16)


def draw_cache_keys(key, part):
    width = KV_HEADS * HEAD
    drawn = jnp.clip(jax.random.normal(key, (R, CL, width), jnp.float32), -6.0, 6.0)
    return drawn.astype(jnp.bfloat16)


def block_scale(key, shape, shards, smallest, largest):
    loudness = 1.0
    for axis_at, shards_of in shards:
        steps = jax.random.uniform(jax.random.fold_in(jax.random.fold_in(key, 6), axis_at), (shards_of,), jnp.float32, smallest / len(shards), largest / len(shards))
        loudness = loudness * jnp.repeat(jnp.exp(steps), shape[axis_at] // shards_of).reshape((-1,) + (1,) * (len(shape) - 1 - axis_at))
    return loudness


def centred(key, shape, scale, limit, pieces=(), held_as=jnp.bfloat16):
    loudness = block_scale(key, shape, pieces, -0.22, 0.18) if pieces else 1.0
    result = jax.random.normal(key, shape, jnp.float32) * scale * loudness
    return jnp.minimum(jnp.maximum(result, -limit), limit).astype(held_as)


def setup_inputs(seed: int = 0) -> dict:
    key_of = jax.random.split(jax.random.key(seed), 10)
    prompt_states = draw_prompt_states(jax.random.fold_in(key_of[9], 71), 0)
    stretch_slot = draw_stretch_slot(jax.random.fold_in(key_of[9], 71), 0)
    cache_length = draw_cache_length(jax.random.fold_in(key_of[9], 71), 0)
    cache_keys = draw_cache_keys(jax.random.fold_in(key_of[9], 71), 0)
    cache_values = centred(key_of[4], (R, CL, KV_HEADS * HEAD), 1.0, 6.0, ((0, 32),))
    step_states = centred(key_of[5], (STEPS, R, D), 1.0, 6.0, ((1, 32),))
    query_weight = centred(key_of[6], (D, HEADS * HEAD), D ** -0.5, 0.0625, ((1, 8),))
    key_weight = centred(key_of[7], (D, KV_HEADS * HEAD), D ** -0.5, 0.0625, ((1, 8),))
    value_weight = centred(key_of[8], (D, KV_HEADS * HEAD), D ** -0.5, 0.0625, ((1, 8),))
    return dict(prompt_states=prompt_states, stretch_slot=stretch_slot, cache_length=cache_length, cache_keys=cache_keys, cache_values=cache_values, step_states=step_states, query_weight=query_weight, key_weight=key_weight, value_weight=value_weight)


rope_base = 500000.0
negative_fill = -1e+30

def frequencies(half):
    indices = jnp.arange(half, dtype=jnp.float32)
    inverse = rope_base ** (-2.0 * indices / (2.0 * half))
    wavelength = 2.0 * math.pi / inverse
    blend = (8192.0 / wavelength - 1.0) / 3.0
    middle = (1.0 - blend) * inverse / 8.0 + blend * inverse
    scaled = jnp.where(wavelength > 8192.0, inverse / 8.0, inverse)
    inside = (wavelength >= 2048.0) & (wavelength <= 8192.0)
    return jnp.where(inside, middle, scaled)

def rotate(values, positions):
    half = values.shape[-1] // 2
    angles = positions.astype(jnp.float32)[..., None, None] * frequencies(half)
    cosine = jnp.cos(angles)
    sine = jnp.sin(angles)
    upper = values[..., :half].astype(jnp.float32)
    lower = values[..., half:].astype(jnp.float32)
    return jnp.concatenate([upper * cosine - lower * sine, lower * cosine + upper * sine], axis=-1)

def run_positions(slots, span):
    indices = jnp.arange(slots.shape[0], dtype=jnp.int32)
    previous = jnp.concatenate([slots[:1] - 1, slots[:-1]])
    opening = (slots != previous) | (indices % span == 0)
    starts = lax.cummax(jnp.where(opening, indices, 0), axis=0)
    return indices - starts

def normalize(scores):
    peak = lax.optimization_barrier(jnp.max(scores, axis=-1, keepdims=True))
    raised = jnp.exp(scores - peak)
    return (raised / lax.optimization_barrier(jnp.sum(raised, axis=-1, keepdims=True))).astype(jnp.bfloat16)

def prompt_group(queries, key_rows, value_rows, slots):
    row_count = queries.shape[0]
    grouped = queries.reshape(row_count, KV_HEADS, HEADS // KV_HEADS, HEAD).astype(jnp.float32)
    scores = jnp.einsum('qkgd,lkd->kgql', grouped, key_rows.astype(jnp.float32)) * (1.0 / math.sqrt(HEAD))
    indices = jnp.arange(row_count, dtype=jnp.int32)
    allowed = (slots[:, None] == slots[None, :]) & (indices[None, :] <= indices[:, None])
    weights = normalize(jnp.where(allowed, scores, negative_fill))
    context = jnp.einsum('kgql,lkd->qkgd', weights.astype(jnp.float32), value_rows.astype(jnp.float32))
    return context.reshape(row_count, HEADS * HEAD).astype(jnp.bfloat16)

def decode_slot(items):
    queries, cache_k, cache_v, prompt_k, prompt_v, recent_k, recent_v, valid = items
    key_all = jnp.concatenate([cache_k, prompt_k, recent_k], axis=0)
    value_all = jnp.concatenate([cache_v, prompt_v, recent_v], axis=0)
    key_all = key_all.reshape(key_all.shape[0], KV_HEADS, HEAD).astype(jnp.float32)
    value_all = value_all.reshape(value_all.shape[0], KV_HEADS, HEAD).astype(jnp.float32)
    grouped = queries.reshape(KV_HEADS, HEADS // KV_HEADS, HEAD).astype(jnp.float32)
    scores = jnp.einsum('kgd,lkd->kgl', grouped, key_all) * (1.0 / math.sqrt(HEAD))
    weights = normalize(jnp.where(valid[None, None, :], scores, negative_fill))
    context = jnp.einsum('kgl,lkd->kgd', weights.astype(jnp.float32), value_all)
    return context.reshape(HEADS * HEAD).astype(jnp.bfloat16)

def reference(prompt_states, stretch_slot, cache_length, cache_keys, cache_values, step_states, query_weight, key_weight, value_weight):
    kv_width = KV_HEADS * HEAD
    all_rows = stretch_slot.shape[0]
    query_raw = jnp.dot(prompt_states, query_weight, preferred_element_type=jnp.float32).astype(jnp.bfloat16)
    key_raw = jnp.dot(prompt_states, key_weight, preferred_element_type=jnp.float32).astype(jnp.bfloat16)
    value_rows = jnp.dot(prompt_states, value_weight, preferred_element_type=jnp.float32).astype(jnp.bfloat16)
    positions = run_positions(stretch_slot, PT)
    queries = rotate(query_raw.reshape(all_rows, HEADS, HEAD), positions).astype(jnp.bfloat16)
    key_rows = rotate(key_raw.reshape(all_rows, KV_HEADS, HEAD), positions).astype(jnp.bfloat16)
    value_heads = value_rows.reshape(all_rows, KV_HEADS, HEAD)

    def one_group(group_index):
        anchor = (group_index * PT).astype(jnp.int32)
        return prompt_group(lax.dynamic_slice_in_dim(queries, anchor, PT, 0), lax.dynamic_slice_in_dim(key_rows, anchor, PT, 0), lax.dynamic_slice_in_dim(value_heads, anchor, PT, 0), lax.dynamic_slice_in_dim(stretch_slot, anchor, PT, 0))
    prompt_out = lax.map(one_group, jnp.arange(N_POOL, dtype=jnp.int32)).reshape(all_rows, HEADS * HEAD)
    every_slot = jnp.arange(R, dtype=jnp.int32)
    matches = stretch_slot[None, :] == every_slot[:, None]
    counts = lax.optimization_barrier(jnp.sum(matches, axis=1)).astype(jnp.int32)
    begins = lax.optimization_barrier(jnp.min(jnp.where(matches, jnp.arange(all_rows, dtype=jnp.int32)[None, :], all_rows), axis=1))
    offsets = jnp.arange(PMAX, dtype=jnp.int32)
    row_ids = jnp.clip(begins[:, None] + offsets[None, :], 0, all_rows - 1)
    prompt_keys = jnp.take(key_rows.reshape(all_rows, kv_width), row_ids, axis=0)
    prompt_values = jnp.take(value_rows, row_ids, axis=0)
    recent_keys = jnp.zeros((R, STEPS, kv_width), jnp.bfloat16)
    recent_values = jnp.zeros((R, STEPS, kv_width), jnp.bfloat16)
    cache_live = jnp.arange(CL, dtype=jnp.int32)[None, :] < cache_length[:, None]
    prompt_live = offsets[None, :] < counts[:, None]
    results = []
    for step_index in range(STEPS):
        states = step_states[step_index]
        step_query_raw = jnp.dot(states, query_weight, preferred_element_type=jnp.float32).astype(jnp.bfloat16)
        step_key_raw = jnp.dot(states, key_weight, preferred_element_type=jnp.float32).astype(jnp.bfloat16)
        step_value = jnp.dot(states, value_weight, preferred_element_type=jnp.float32).astype(jnp.bfloat16)
        moment = cache_length + counts + step_index
        step_query = rotate(step_query_raw.reshape(R, HEADS, HEAD), moment).astype(jnp.bfloat16)
        step_key = rotate(step_key_raw.reshape(R, KV_HEADS, HEAD), moment).astype(jnp.bfloat16).reshape(R, kv_width)
        recent_keys = recent_keys.at[:, step_index].set(step_key)
        recent_values = recent_values.at[:, step_index].set(step_value)
        recent_live = jnp.broadcast_to(jnp.arange(STEPS, dtype=jnp.int32)[None, :] <= step_index, (R, STEPS))
        valid = jnp.concatenate([cache_live, prompt_live, recent_live], axis=1)
        results.append(lax.map(decode_slot, (step_query, cache_keys, cache_values, prompt_keys, prompt_values, recent_keys, recent_values, valid)))
    step_out = jnp.stack(results, axis=0)
    return (prompt_out, step_out)
```

```python
import functools
import math

import jax
import jax.numpy as jnp
from jax import lax
from jax.experimental import pallas as pl
from jax.experimental.pallas import tpu as pltpu
from jax.sharding import PartitionSpec as P

HEADS = 64
KV_HEADS = 8
HEAD = 128
PMAX = 32
STEPS = 4


rope_base = 500000.0
negative_fill = -1e30


def frequencies(half):
    indices = jnp.arange(half, dtype=jnp.float32)
    inverse = rope_base ** (-2.0 * indices / (2.0 * half))
    wavelength = 2.0 * math.pi / inverse
    blend = (8192.0 / wavelength - 1.0) / 3.0
    middle = (1.0 - blend) * inverse / 8.0 + blend * inverse
    scaled = jnp.where(wavelength > 8192.0, inverse / 8.0, inverse)
    inside = (wavelength >= 2048.0) & (wavelength <= 8192.0)
    return jnp.where(inside, middle, scaled)


def rotate(values, positions):
    half = values.shape[-1] // 2
    angles = positions.astype(jnp.float32)[..., None, None] * frequencies(half)
    cosine = jnp.cos(angles)
    sine = jnp.sin(angles)
    upper = values[..., :half].astype(jnp.float32)
    lower = values[..., half:].astype(jnp.float32)
    return jnp.concatenate([upper * cosine - lower * sine, lower * cosine + upper * sine], axis=-1)


def run_positions(slots, span):
    indices = jnp.arange(slots.shape[0], dtype=jnp.int32)
    previous = jnp.concatenate([slots[:1] - 1, slots[:-1]])
    opening = (slots != previous) | (indices % span == 0)
    starts = lax.cummax(jnp.where(opening, indices, 0), axis=0)
    return indices - starts


def normalize(scores):
    peak = jnp.max(scores, axis=-1, keepdims=True)
    raised = jnp.exp(scores - peak)
    return (raised / jnp.sum(raised, axis=-1, keepdims=True)).astype(jnp.bfloat16)


def project(states, query_weight, key_weight, value_weight):
    products = [
        jnp.dot(states, weight, preferred_element_type=jnp.float32)
        for weight in (query_weight, key_weight, value_weight)
    ]
    return jnp.concatenate(products, axis=1).astype(jnp.bfloat16)


def decode_attend(queries, blocks, scale):
    slot_count = queries.shape[0]
    grouped = queries.reshape(slot_count, KV_HEADS, HEADS // KV_HEADS, HEAD)
    score_blocks = []
    for key_block, value_block, live_rows in blocks:
        key_heads = key_block.reshape(slot_count, key_block.shape[1], KV_HEADS, HEAD)
        scores = (
            jnp.einsum("rkgd,rlkd->rkgl", grouped, key_heads, preferred_element_type=jnp.float32)
            * scale
        )
        score_blocks.append(jnp.where(live_rows[:, None, None, :], scores, negative_fill))
    weights = normalize(jnp.concatenate(score_blocks, axis=-1))
    context = jnp.zeros((slot_count, KV_HEADS, HEADS // KV_HEADS, HEAD), jnp.float32)
    position = 0
    for key_block, value_block, live_rows in blocks:
        extent = value_block.shape[1]
        shares = weights[..., position : position + extent]
        value_heads = value_block.reshape(slot_count, extent, KV_HEADS, HEAD)
        context = context + jnp.einsum(
            "rkgl,rlkd->rkgd", shares, value_heads, preferred_element_type=jnp.float32
        )
        position = position + extent
    return context.reshape(slot_count, HEADS * HEAD).astype(jnp.bfloat16)


def on_device(
    prompt_states,
    stretch_slot,
    cache_length,
    cache_keys,
    cache_values,
    step_states,
    query_weight,
    key_weight,
    value_weight,
):
    pool_index = lax.axis_index("pool")
    tp_index = lax.axis_index("tp")
    tp_count = lax.axis_size("tp")
    query_width = query_weight.shape[1]
    column_width = key_weight.shape[1]
    kv_width = KV_HEADS * HEAD
    local_heads = query_width // HEAD
    group_size = HEADS // KV_HEADS
    scale = 1.0 / math.sqrt(HEAD)
    projected = project(
        lax.all_gather(prompt_states, "tp", axis=0, tiled=True),
        query_weight,
        key_weight,
        value_weight,
    )
    stretch_rows = projected.shape[0]
    query_raw = projected[:, :query_width]
    key_part = projected[:, query_width : query_width + column_width]
    value_part = projected[:, query_width + column_width :]
    key_raw, value_rows = (
        lax.all_gather(key_part, "tp", axis=1, tiled=True),
        lax.all_gather(value_part, "tp", axis=1, tiled=True),
    )
    group_slots = lax.dynamic_slice_in_dim(stretch_slot, pool_index * stretch_rows, stretch_rows, 0)
    positions = run_positions(group_slots, stretch_rows)
    queries = rotate(query_raw.reshape(stretch_rows, local_heads, HEAD), positions).astype(
        jnp.bfloat16
    )
    key_rows = rotate(key_raw.reshape(stretch_rows, KV_HEADS, HEAD), positions).astype(jnp.bfloat16)
    kv_index = tp_index * local_heads // group_size
    key_head = lax.dynamic_index_in_dim(key_rows, kv_index, 1, keepdims=False)
    value_head = lax.dynamic_index_in_dim(
        value_rows.reshape(stretch_rows, KV_HEADS, HEAD), kv_index, 1, keepdims=False
    )
    scores = (
        jnp.einsum("qhd,ld->hql", queries, key_head, preferred_element_type=jnp.float32) * scale
    )
    indices = jnp.arange(stretch_rows, dtype=jnp.int32)
    allowed = (group_slots[:, None] == group_slots[None, :]) & (
        indices[None, :] <= indices[:, None]
    )
    weights = normalize(jnp.where(allowed[None], scores, negative_fill))
    context = jnp.einsum("hql,ld->qhd", weights, value_head, preferred_element_type=jnp.float32)
    prompt_out = context.reshape(stretch_rows, query_width).astype(jnp.bfloat16)
    kv_pair = jnp.concatenate([key_rows.reshape(stretch_rows, kv_width), value_rows], axis=1)
    slot_count = cache_length.shape[0]
    device_index = pool_index * tp_count + tp_index
    my_slots = device_index * slot_count + jnp.arange(slot_count, dtype=jnp.int32)
    all_rows = stretch_slot.shape[0]
    all_indices = jnp.arange(all_rows, dtype=jnp.int32)
    matches = stretch_slot[None, :] == my_slots[:, None]
    counts = jnp.sum(matches, axis=1)
    offsets = jnp.arange(PMAX, dtype=jnp.int32)
    everything = lax.all_gather(kv_pair, "pool", axis=0, tiled=True)
    begins = jnp.min(jnp.where(matches, all_indices[None, :], all_rows), axis=1)
    row_ids = jnp.clip(begins[:, None] + offsets[None, :], 0, all_rows - 1)
    prompt_pair = jnp.take(everything, row_ids.reshape(-1), axis=0).reshape(
        slot_count, PMAX, 2 * kv_width
    )
    prompt_keys = prompt_pair[:, :, :kv_width]
    prompt_values = prompt_pair[:, :, kv_width:]
    recent_keys = jnp.zeros((slot_count, STEPS, kv_width), jnp.bfloat16)
    recent_values = jnp.zeros((slot_count, STEPS, kv_width), jnp.bfloat16)
    cache_live = jnp.arange(cache_keys.shape[1], dtype=jnp.int32)[None, :] < cache_length[:, None]
    prompt_live = offsets[None, :] < counts[:, None]
    step_indices = jnp.arange(STEPS, dtype=jnp.int32)
    section = lax.all_gather(step_states, "tp", axis=1, tiled=True)
    step_count = section.shape[0]
    row_count = section.shape[1]
    flat = project(
        section.reshape(step_count * row_count, section.shape[2]),
        query_weight,
        key_weight,
        value_weight,
    )
    every_projected = flat.reshape(step_count, row_count, flat.shape[1])
    query_every, key_every, value_every = (
        lax.all_to_all(
            every_projected[:, :, :query_width], "tp", split_axis=1, concat_axis=2, tiled=True
        ),
        lax.all_to_all(
            every_projected[:, :, query_width : query_width + column_width],
            "tp",
            split_axis=1,
            concat_axis=2,
            tiled=True,
        ),
        lax.all_to_all(
            every_projected[:, :, query_width + column_width :],
            "tp",
            split_axis=1,
            concat_axis=2,
            tiled=True,
        ),
    )
    results = []
    for step_index in range(STEPS):
        query_slot = query_every[step_index]
        key_slot = key_every[step_index]
        value_slot = value_every[step_index]
        moment = cache_length + counts + step_index
        step_query = rotate(query_slot.reshape(slot_count, HEADS, HEAD), moment).astype(
            jnp.bfloat16
        )
        step_key = (
            rotate(key_slot.reshape(slot_count, KV_HEADS, HEAD), moment)
            .astype(jnp.bfloat16)
            .reshape(slot_count, kv_width)
        )
        recent_keys = recent_keys.at[:, step_index].set(step_key)
        recent_values = recent_values.at[:, step_index].set(value_slot)
        recent_live = jnp.broadcast_to(step_indices[None, :] <= step_index, (slot_count, STEPS))
        blocks = (
            (cache_keys, cache_values, cache_live),
            (prompt_keys, prompt_values, prompt_live),
            (recent_keys, recent_values, recent_live),
        )
        results.append(decode_attend(step_query, blocks, scale))
    step_out = jnp.stack(results, axis=0)
    return (prompt_out, step_out)


CHUNKS = 8
MESH = pl.DeviceIdType.MESH
VMEM_LIMIT = 60000 * 1024


def greet(targets):
    barrier = pltpu.get_barrier_semaphore()
    for target in targets:
        pl.semaphore_signal(barrier, inc=1, device_id=target, device_id_type=MESH)
    pl.semaphore_wait(barrier, len(targets))


def project_kernel(
    count, prompt_ref, step_ref, wq_ref, wk_ref, wv_ref,
    pq_ref, pk_ref, pv_ref, sq_ref, sk_ref, sv_ref,
    rows_p, rows_s, vq, vk, vv, acc_q, acc_k, acc_v,
    own_sem, weight_sem, send_sem, recv_sem,
):
    pool = lax.axis_index("pool")
    me = lax.axis_index("tp")
    core = lax.rem(me, 2)

    def around(start, shift):
        return lax.rem(start + shift + count, count)

    partner = me + 1 - 2 * core
    left, right, opposite = around(me, -2), around(me, 2), around(me, 4)
    width = prompt_ref.shape[1] // CHUNKS
    bufs = (rows_p, rows_s)

    def cols(k):
        return pl.ds(k * width, width)

    own = []
    for k in range(CHUNKS):
        for b, source in enumerate((prompt_ref, step_ref)):
            copy = pltpu.make_async_copy(
                source.at[:, cols(k)], bufs[b].at[me, :, cols(k)], own_sem.at[b, k]
            )
            copy.start()
            own.append(copy)
    weights = []
    for k in range(CHUNKS):
        for j, (source, target) in enumerate(((wq_ref, vq), (wk_ref, vk), (wv_ref, vv))):
            copy = pltpu.make_async_copy(source.at[cols(k)], target.at[cols(k)], weight_sem.at[j, k])
            copy.start()
            weights.append(copy)
    greet([(pool, left), (pool, right), (pool, partner)])
    acc_q[...] = jnp.zeros_like(acc_q)
    acc_k[...] = jnp.zeros_like(acc_k)
    acc_v[...] = jnp.zeros_like(acc_v)
    sent = []

    def transfer(b, slot, k, kind, target):
        place = bufs[b].at[slot, :, cols(k)]
        return pltpu.make_async_remote_copy(
            src_ref=place,
            dst_ref=place,
            send_sem=send_sem.at[b, kind, k],
            recv_sem=recv_sem.at[b, kind, k],
            device_id=(pool, target),
            device_id_type=MESH,
        )

    def send(slot, k, kind, target):
        for b in range(2):
            copy = transfer(b, slot, k, kind, target)
            copy.start()
            sent.append(copy)

    def arrive(slot, k, kind):
        for b in range(2):
            transfer(b, slot, k, kind, partner).wait_recv()

    for k in range(CHUNKS):
        own[2 * k].wait()
        own[2 * k + 1].wait()
        send(me, k, 0, right)
        send(me, k, 1, left)
        send(me, k, 3, partner)

    def relay_near(k):
        arrive(left, k, 0)
        if k % 2 == 0:
            send(left, k, 2, right)
        send(left, k, 4, partner)
        arrive(right, k, 1)
        if k % 2 == 1:
            send(right, k, 2, left)
        send(right, k, 5, partner)

    def relay_far(k):
        arrive(opposite, k, 2)
        send(opposite, k, 6, partner)

    def multiply(k):
        arrive(partner, k, 3)
        arrive(around(partner, -2), k, 4)
        arrive(around(partner, 2), k, 5)
        arrive(around(partner, 4), k, 6)
        for j in range(3):
            weights[3 * k + j].wait()
        left_p = rows_p[:, :, cols(k)].reshape(-1, width)
        left_s = rows_s[:, :, cols(k)].astype(jnp.float32).reshape(-1, width).astype(jnp.bfloat16)
        lhs = jnp.concatenate([left_p, left_s], axis=0)
        for vref, acc in ((vq, acc_q), (vk, acc_k), (vv, acc_v)):
            acc[...] += jnp.dot(lhs, vref[cols(k), :], preferred_element_type=jnp.float32)

    for k in range(CHUNKS + 2):
        if k < CHUNKS:
            relay_near(k)
        if 1 <= k <= CHUNKS:
            relay_far(k - 1)
        if k >= 2:
            multiply(k - 2)
    split = pq_ref.shape[0]
    for acc, p_ref, s_ref in ((acc_q, pq_ref, sq_ref), (acc_k, pk_ref, sk_ref), (acc_v, pv_ref, sv_ref)):
        p_ref[...] = acc[:split].astype(jnp.bfloat16)
        s_ref[...] = acc[split:].astype(jnp.bfloat16)
    for copy in sent:
        copy.wait_send()


def gather_project(prompt, step, wq, wk, wv, count):
    depth = prompt.shape[1]
    prompt_rows, step_rows = prompt.shape[0], step.shape[0]
    widths = (wq.shape[1], wk.shape[1], wv.shape[1])
    anywhere = pl.BlockSpec(memory_space=pl.ANY)
    inside = pl.BlockSpec(memory_space=pltpu.VMEM)
    total = count * (prompt_rows + step_rows)
    return pl.pallas_call(
        functools.partial(project_kernel, count),
        out_shape=[jax.ShapeDtypeStruct((count * prompt_rows, w), jnp.bfloat16) for w in widths]
        + [jax.ShapeDtypeStruct((count * step_rows, w), jnp.bfloat16) for w in widths],
        in_specs=[anywhere] * 5,
        out_specs=[inside] * 6,
        scratch_shapes=[
            pltpu.VMEM((count, prompt_rows, depth), jnp.bfloat16),
            pltpu.VMEM((count, step_rows, depth), jnp.bfloat16),
        ]
        + [pltpu.VMEM((depth, w), jnp.bfloat16) for w in widths]
        + [pltpu.VMEM((total, w), jnp.float32) for w in widths]
        + [
            pltpu.SemaphoreType.DMA((2, CHUNKS)),
            pltpu.SemaphoreType.DMA((3, CHUNKS)),
            pltpu.SemaphoreType.DMA((2, 7, CHUNKS)),
            pltpu.SemaphoreType.DMA((2, 7, CHUNKS)),
        ],
        compiler_params=pltpu.CompilerParams(
            collective_id=0, has_side_effects=True, vmem_limit_bytes=VMEM_LIMIT
        ),
    )(prompt, step, wq, wk, wv)


def nt(a, b):
    return lax.dot_general(a, b, (((1,), (1,)), ((), ())), preferred_element_type=jnp.float32)


def attend_kernel(
    pools, count, real_rows, scale,
    pq_ref, pk_ref, pv_ref, sq_ref, sk_ref, sv_ref,
    all_slots_ref, slot_col_ref, slot_row_ref, freq_ref, length_ref,
    cache_k_ref, cache_v_ref,
    out_ref, step_out_ref,
    pairs, outgoing, incoming, ck, cv,
    cache_sem, pool_send, pool_recv, tp_send, tp_recv,
):
    pool = lax.axis_index("pool")
    me = lax.axis_index("tp")
    f32, bf16 = jnp.float32, jnp.bfloat16
    heads = pq_ref.shape[1] // HEAD
    caches = [
        pltpu.make_async_copy(cache_k_ref, ck, cache_sem.at[0]),
        pltpu.make_async_copy(cache_v_ref, cv, cache_sem.at[1]),
    ]
    for copy in caches:
        copy.start()
    peers = [lax.rem(pool + d, pools) for d in range(1, pools)]
    mates = [lax.rem(me + d, count) for d in range(1, count)]
    greet([(peer, me) for peer in peers] + [(pool, mate) for mate in mates])
    sign = jnp.where(lax.broadcasted_iota(jnp.int32, (1, HEAD), 1) < HEAD // 2, -1.0, 1.0)
    freq = freq_ref[...]

    def tables(position):
        angles = position.astype(f32) * freq
        return jnp.cos(angles), jnp.sin(angles) * sign

    def turn(values, table):
        return values * table[0] + pltpu.roll(values, HEAD // 2, 1) * table[1]

    rows = pq_ref.shape[0]
    row_at = lax.broadcasted_iota(jnp.int32, (rows, rows), 0)
    col_at = lax.broadcasted_iota(jnp.int32, (rows, rows), 1)
    allowed = (slot_col_ref[...] == slot_row_ref[...]) & (col_at <= row_at)
    position = jnp.sum(allowed.astype(f32), axis=1, keepdims=True) - 1.0
    table = tables(position)
    key_rows = turn(pk_ref[...].astype(f32), table).astype(bf16)
    value_rows = pv_ref[...]
    pairs[pool, :, :HEAD] = key_rows
    pairs[pool, :, HEAD:] = value_rows
    sent = []
    for d, peer in enumerate(peers):
        copy = pltpu.make_async_remote_copy(
            src_ref=pairs.at[pool],
            dst_ref=pairs.at[pool],
            send_sem=pool_send.at[d],
            recv_sem=pool_recv.at[d],
            device_id=(peer, me),
            device_id_type=MESH,
        )
        copy.start()
        sent.append(copy)
    blocks = rows // count
    for h in range(heads):
        lanes = slice(h * HEAD, (h + 1) * HEAD)
        query = turn(pq_ref[:, lanes].astype(f32), table).astype(bf16)
        scores = jnp.where(allowed, nt(query, key_rows) * scale, negative_fill)
        raised = jnp.exp(scores - jnp.max(scores, axis=1, keepdims=True))
        weights = (raised / jnp.sum(raised, axis=1, keepdims=True)).astype(bf16)
        context = jnp.dot(weights, value_rows, preferred_element_type=f32).astype(bf16)
        for t in range(count):
            out_ref[t * real_rows : (t + 1) * real_rows, lanes] = context[
                t * blocks : t * blocks + real_rows
            ]
    step_rows = sq_ref.shape[0]
    block = step_rows // count
    local = block // STEPS
    first = pool * count * local

    def row_slot(index):
        return first + (index // block) * local + lax.rem(index, local)

    def row_step(index):
        return lax.rem(index, block) // local

    index_col = lax.broadcasted_iota(jnp.int32, (step_rows, 1), 0)
    index_row = lax.broadcasted_iota(jnp.int32, (1, step_rows), 1)
    all_slots = all_slots_ref[...]
    match = all_slots == row_slot(index_col)
    tally = jnp.sum(match.astype(f32), axis=1, keepdims=True)
    named = tally > 0.0
    moment = jnp.where(named, tally + row_step(index_col).astype(f32), 0.0)
    step_table = tables(moment)
    step_key = turn(sk_ref[...].astype(f32), step_table)
    step_value = sv_ref[...]
    step_key_rows = step_key.astype(bf16)
    recent = (row_slot(index_col) == row_slot(index_row)) & (
        row_step(index_row) <= row_step(index_col)
    )
    for d in range(1, pools):
        source = lax.rem(pool + pools - d, pools)
        pltpu.make_async_remote_copy(
            src_ref=pairs.at[source],
            dst_ref=pairs.at[source],
            send_sem=pool_send.at[d - 1],
            recv_sem=pool_recv.at[d - 1],
            device_id=(peers[d - 1], me),
            device_id_type=MESH,
        ).wait_recv()
    prompt_keys = pairs[:, :, :HEAD].reshape(-1, HEAD)
    prompt_values = pairs[:, :, HEAD:].reshape(-1, HEAD)

    def pack(lanes, values):
        outgoing[:, :, lanes] = values.reshape(count, block, HEAD).astype(bf16)

    for h in range(heads):
        lanes = slice(h * HEAD, (h + 1) * HEAD)
        turned = turn(sq_ref[:, lanes].astype(f32), step_table)
        query = turned.astype(bf16)
        far = jnp.where(match, nt(query, prompt_keys) * scale, negative_fill)
        near = jnp.where(recent, nt(query, step_key_rows) * scale, negative_fill)
        peak = jnp.maximum(
            jnp.max(far, axis=1, keepdims=True), jnp.max(near, axis=1, keepdims=True)
        )
        far, near = jnp.exp(far - peak), jnp.exp(near - peak)
        bottom = jnp.sum(far, axis=1, keepdims=True) + jnp.sum(near, axis=1, keepdims=True)
        context = jnp.dot(
            (far / bottom).astype(bf16), prompt_values, preferred_element_type=f32
        ) + jnp.dot((near / bottom).astype(bf16), step_value, preferred_element_type=f32)
        pack(lanes, jnp.where(named, context, turned))
    wide = heads * HEAD
    pack(slice(wide, wide + HEAD), step_key)
    pack(slice(wide + HEAD, wide + 2 * HEAD), step_value.astype(f32))
    for d, mate in enumerate(mates):
        copy = pltpu.make_async_remote_copy(
            src_ref=outgoing.at[mate],
            dst_ref=incoming.at[me],
            send_sem=tp_send.at[d],
            recv_sem=tp_recv.at[d],
            device_id=(pool, mate),
            device_id_type=MESH,
        )
        copy.start()
        sent.append(copy)
    incoming[me] = outgoing[me]
    own_col = lax.broadcasted_iota(jnp.int32, (block, 1), 0)
    own_slot = first + me * local + lax.rem(own_col, local)
    own_named = jnp.sum((all_slots == own_slot).astype(f32), axis=1, keepdims=True) > 0.0
    lengths = length_ref[...]
    own_table = tables((lengths + own_col // local).astype(f32))
    many = heads * block
    many_col = lax.rem(lax.broadcasted_iota(jnp.int32, (many, 1), 0), block)
    block_row = lax.broadcasted_iota(jnp.int32, (1, block), 1)
    own_recent = (lax.rem(many_col, local) == lax.rem(block_row, local)) & (
        block_row // local <= many_col // local
    )
    many_lengths = jnp.concatenate([lengths] * heads, axis=0)
    extent = ck.shape[1]
    cache_at = lax.broadcasted_iota(jnp.int32, (1, extent), 1)
    live = [
        cache_at < jnp.where(lax.rem(many_col, local) == s, many_lengths, 0) for s in range(local)
    ]
    for copy in caches:
        copy.wait()
    for d in range(1, count):
        source = lax.rem(me + count - d, count)
        pltpu.make_async_remote_copy(
            src_ref=outgoing.at[source],
            dst_ref=incoming.at[source],
            send_sem=tp_send.at[d - 1],
            recv_sem=tp_recv.at[d - 1],
            device_id=(pool, mates[d - 1]),
            device_id_type=MESH,
        ).wait_recv()
    for t in range(count):
        got = incoming[t].astype(f32)
        query = jnp.concatenate(
            [turn(got[:, h * HEAD : (h + 1) * HEAD], own_table) for h in range(heads)], axis=0
        ).astype(bf16)
        key = turn(got[:, wide : wide + HEAD], own_table).astype(bf16)
        value = got[:, wide + HEAD :].astype(bf16)
        lanes = slice(t * HEAD, (t + 1) * HEAD)
        parts = [
            jnp.where(live[s], nt(query, ck[s, :, lanes]) * scale, negative_fill)
            for s in range(local)
        ]
        parts.append(jnp.where(own_recent, nt(query, key) * scale, negative_fill))
        peak = functools.reduce(
            jnp.maximum, [jnp.max(part, axis=1, keepdims=True) for part in parts]
        )
        parts = [jnp.exp(part - peak) for part in parts]
        bottom = sum(jnp.sum(part, axis=1, keepdims=True) for part in parts)
        shares = [(part / bottom).astype(bf16) for part in parts]
        context = jnp.dot(shares[-1], value, preferred_element_type=f32)
        for s in range(local):
            context = context + jnp.dot(
                shares[s], cv[s, :, lanes], preferred_element_type=f32
            )
        for h in range(heads):
            at = slice((t * heads + h) * HEAD, (t * heads + h + 1) * HEAD)
            step_out_ref[:, at] = jnp.where(
                own_named,
                got[:, h * HEAD : (h + 1) * HEAD],
                context[h * block : (h + 1) * block],
            ).astype(bf16)
    for copy in sent:
        copy.wait_send()


def fast_device(
    pools, prompt_states, stretch_slot, cache_length, cache_keys, cache_values, step_states,
    query_weight, key_weight, value_weight,
):
    count = lax.axis_size("tp")
    pool = lax.axis_index("pool")
    real_rows = prompt_states.shape[0]
    padded = -(-real_rows // 16) * 16
    prompt = jnp.pad(prompt_states, ((0, padded - real_rows), (0, 0)))
    local = cache_length.shape[0]
    step = step_states.reshape(STEPS * local, step_states.shape[2])
    projected = gather_project(prompt, step, query_weight, key_weight, value_weight, count)
    slots = jnp.pad(
        stretch_slot.reshape(pools, count, real_rows),
        ((0, 0), (0, 0), (0, padded - real_rows)),
        constant_values=-1,
    ).reshape(pools, count * padded)
    mine = lax.dynamic_slice_in_dim(slots, pool, 1, 0)
    half = frequencies(HEAD // 2)
    freq = jnp.concatenate([half, half])[None, :]
    lengths = jnp.tile(cache_length, STEPS)[:, None]
    inside = pl.BlockSpec(memory_space=pltpu.VMEM)
    anywhere = pl.BlockSpec(memory_space=pl.ANY)
    width = query_weight.shape[1]
    block = STEPS * local
    prompt_out, step_out = pl.pallas_call(
        functools.partial(attend_kernel, pools, count, real_rows, 1.0 / math.sqrt(HEAD)),
        out_shape=[
            jax.ShapeDtypeStruct((count * real_rows, width), jnp.bfloat16),
            jax.ShapeDtypeStruct((block, count * width), jnp.bfloat16),
        ],
        in_specs=[inside] * 11 + [anywhere] * 2,
        out_specs=[inside] * 2,
        scratch_shapes=[
            pltpu.VMEM((pools, count * padded, 2 * HEAD), jnp.bfloat16),
            pltpu.VMEM((count, block, width + 2 * HEAD), jnp.bfloat16),
            pltpu.VMEM((count, block, width + 2 * HEAD), jnp.bfloat16),
            pltpu.VMEM(cache_keys.shape, jnp.bfloat16),
            pltpu.VMEM(cache_values.shape, jnp.bfloat16),
            pltpu.SemaphoreType.DMA((2,)),
            pltpu.SemaphoreType.DMA((pools - 1,)),
            pltpu.SemaphoreType.DMA((pools - 1,)),
            pltpu.SemaphoreType.DMA((count - 1,)),
            pltpu.SemaphoreType.DMA((count - 1,)),
        ],
        compiler_params=pltpu.CompilerParams(
            collective_id=1, has_side_effects=True, vmem_limit_bytes=VMEM_LIMIT
        ),
    )(
        *projected, slots.reshape(1, -1), mine.reshape(-1, 1), mine, freq, lengths,
        cache_keys, cache_values,
    )
    return prompt_out, step_out.reshape(STEPS, local, count * width)


def per_device(pools, *args):
    count = lax.axis_size("tp")
    if count == KV_HEADS and args[7].shape[1] == HEAD and (args[2].shape[0] * STEPS) % 8 == 0:
        return fast_device(pools, *args)
    return on_device(*args)


def solution(mesh):
    in_specs = (
        P(("pool", "tp"), None),
        P(),
        P(("pool", "tp")),
        P(("pool", "tp"), None, None),
        P(("pool", "tp"), None, None),
        P(None, ("pool", "tp"), None),
        P(None, "tp"),
        P(None, "tp"),
        P(None, "tp"),
    )
    out_specs = (P("pool", "tp"), P(None, ("pool", "tp"), None))
    return jax.shard_map(
        functools.partial(per_device, mesh.shape["pool"]), mesh=mesh, in_specs=in_specs, out_specs=out_specs, check_vma=False
    )
```

```python
import functools
import math

import jax
import jax.numpy as jnp
from jax import lax
from jax.experimental import pallas as pl
from jax.experimental.pallas import tpu as pltpu
from jax.sharding import PartitionSpec as P

HEADS = 64
KV_HEADS = 8
HEAD = 128
PMAX = 32
STEPS = 4


rope_base = 500000.0
negative_fill = -1e30


def frequencies(half):
    indices = jnp.arange(half, dtype=jnp.float32)
    inverse = rope_base ** (-2.0 * indices / (2.0 * half))
    wavelength = 2.0 * math.pi / inverse
    blend = (8192.0 / wavelength - 1.0) / 3.0
    middle = (1.0 - blend) * inverse / 8.0 + blend * inverse
    scaled = jnp.where(wavelength > 8192.0, inverse / 8.0, inverse)
    inside = (wavelength >= 2048.0) & (wavelength <= 8192.0)
    return jnp.where(inside, middle, scaled)


def rotate(values, positions):
    half = values.shape[-1] // 2
    angles = positions.astype(jnp.float32)[..., None, None] * frequencies(half)
    cosine = jnp.cos(angles)
    sine = jnp.sin(angles)
    upper = values[..., :half].astype(jnp.float32)
    lower = values[..., half:].astype(jnp.float32)
    return jnp.concatenate([upper * cosine - lower * sine, lower * cosine + upper * sine], axis=-1)


def run_positions(slots, span):
    indices = jnp.arange(slots.shape[0], dtype=jnp.int32)
    previous = jnp.concatenate([slots[:1] - 1, slots[:-1]])
    opening = (slots != previous) | (indices % span == 0)
    starts = lax.cummax(jnp.where(opening, indices, 0), axis=0)
    return indices - starts


def normalize(scores):
    peak = jnp.max(scores, axis=-1, keepdims=True)
    raised = jnp.exp(scores - peak)
    return (raised / jnp.sum(raised, axis=-1, keepdims=True)).astype(jnp.bfloat16)


def project(states, query_weight, key_weight, value_weight):
    products = [
        jnp.dot(states, weight, preferred_element_type=jnp.float32)
        for weight in (query_weight, key_weight, value_weight)
    ]
    return jnp.concatenate(products, axis=1).astype(jnp.bfloat16)


def decode_attend(queries, blocks, scale):
    slot_count = queries.shape[0]
    grouped = queries.reshape(slot_count, KV_HEADS, HEADS // KV_HEADS, HEAD)
    score_blocks = []
    for key_block, value_block, live_rows in blocks:
        key_heads = key_block.reshape(slot_count, key_block.shape[1], KV_HEADS, HEAD)
        scores = (
            jnp.einsum("rkgd,rlkd->rkgl", grouped, key_heads, preferred_element_type=jnp.float32)
            * scale
        )
        score_blocks.append(jnp.where(live_rows[:, None, None, :], scores, negative_fill))
    weights = normalize(jnp.concatenate(score_blocks, axis=-1))
    context = jnp.zeros((slot_count, KV_HEADS, HEADS // KV_HEADS, HEAD), jnp.float32)
    position = 0
    for key_block, value_block, live_rows in blocks:
        extent = value_block.shape[1]
        shares = weights[..., position : position + extent]
        value_heads = value_block.reshape(slot_count, extent, KV_HEADS, HEAD)
        context = context + jnp.einsum(
            "rkgl,rlkd->rkgd", shares, value_heads, preferred_element_type=jnp.float32
        )
        position = position + extent
    return context.reshape(slot_count, HEADS * HEAD).astype(jnp.bfloat16)


def on_device(
    prompt_states,
    stretch_slot,
    cache_length,
    cache_keys,
    cache_values,
    step_states,
    query_weight,
    key_weight,
    value_weight,
):
    pool_index = lax.axis_index("pool")
    tp_index = lax.axis_index("tp")
    tp_count = lax.axis_size("tp")
    query_width = query_weight.shape[1]
    column_width = key_weight.shape[1]
    kv_width = KV_HEADS * HEAD
    local_heads = query_width // HEAD
    group_size = HEADS // KV_HEADS
    scale = 1.0 / math.sqrt(HEAD)
    projected = project(
        lax.all_gather(prompt_states, "tp", axis=0, tiled=True),
        query_weight,
        key_weight,
        value_weight,
    )
    stretch_rows = projected.shape[0]
    query_raw = projected[:, :query_width]
    key_part = projected[:, query_width : query_width + column_width]
    value_part = projected[:, query_width + column_width :]
    key_raw, value_rows = (
        lax.all_gather(key_part, "tp", axis=1, tiled=True),
        lax.all_gather(value_part, "tp", axis=1, tiled=True),
    )
    group_slots = lax.dynamic_slice_in_dim(stretch_slot, pool_index * stretch_rows, stretch_rows, 0)
    positions = run_positions(group_slots, stretch_rows)
    queries = rotate(query_raw.reshape(stretch_rows, local_heads, HEAD), positions).astype(
        jnp.bfloat16
    )
    key_rows = rotate(key_raw.reshape(stretch_rows, KV_HEADS, HEAD), positions).astype(jnp.bfloat16)
    kv_index = tp_index * local_heads // group_size
    key_head = lax.dynamic_index_in_dim(key_rows, kv_index, 1, keepdims=False)
    value_head = lax.dynamic_index_in_dim(
        value_rows.reshape(stretch_rows, KV_HEADS, HEAD), kv_index, 1, keepdims=False
    )
    scores = (
        jnp.einsum("qhd,ld->hql", queries, key_head, preferred_element_type=jnp.float32) * scale
    )
    indices = jnp.arange(stretch_rows, dtype=jnp.int32)
    allowed = (group_slots[:, None] == group_slots[None, :]) & (
        indices[None, :] <= indices[:, None]
    )
    weights = normalize(jnp.where(allowed[None], scores, negative_fill))
    context = jnp.einsum("hql,ld->qhd", weights, value_head, preferred_element_type=jnp.float32)
    prompt_out = context.reshape(stretch_rows, query_width).astype(jnp.bfloat16)
    kv_pair = jnp.concatenate([key_rows.reshape(stretch_rows, kv_width), value_rows], axis=1)
    slot_count = cache_length.shape[0]
    device_index = pool_index * tp_count + tp_index
    my_slots = device_index * slot_count + jnp.arange(slot_count, dtype=jnp.int32)
    all_rows = stretch_slot.shape[0]
    all_indices = jnp.arange(all_rows, dtype=jnp.int32)
    matches = stretch_slot[None, :] == my_slots[:, None]
    counts = jnp.sum(matches, axis=1)
    offsets = jnp.arange(PMAX, dtype=jnp.int32)
    everything = lax.all_gather(kv_pair, "pool", axis=0, tiled=True)
    begins = jnp.min(jnp.where(matches, all_indices[None, :], all_rows), axis=1)
    row_ids = jnp.clip(begins[:, None] + offsets[None, :], 0, all_rows - 1)
    prompt_pair = jnp.take(everything, row_ids.reshape(-1), axis=0).reshape(
        slot_count, PMAX, 2 * kv_width
    )
    prompt_keys = prompt_pair[:, :, :kv_width]
    prompt_values = prompt_pair[:, :, kv_width:]
    recent_keys = jnp.zeros((slot_count, STEPS, kv_width), jnp.bfloat16)
    recent_values = jnp.zeros((slot_count, STEPS, kv_width), jnp.bfloat16)
    cache_live = jnp.arange(cache_keys.shape[1], dtype=jnp.int32)[None, :] < cache_length[:, None]
    prompt_live = offsets[None, :] < counts[:, None]
    step_indices = jnp.arange(STEPS, dtype=jnp.int32)
    section = lax.all_gather(step_states, "tp", axis=1, tiled=True)
    step_count = section.shape[0]
    row_count = section.shape[1]
    flat = project(
        section.reshape(step_count * row_count, section.shape[2]),
        query_weight,
        key_weight,
        value_weight,
    )
    every_projected = flat.reshape(step_count, row_count, flat.shape[1])
    query_every, key_every, value_every = (
        lax.all_to_all(
            every_projected[:, :, :query_width], "tp", split_axis=1, concat_axis=2, tiled=True
        ),
        lax.all_to_all(
            every_projected[:, :, query_width : query_width + column_width],
            "tp",
            split_axis=1,
            concat_axis=2,
            tiled=True,
        ),
        lax.all_to_all(
            every_projected[:, :, query_width + column_width :],
            "tp",
            split_axis=1,
            concat_axis=2,
            tiled=True,
        ),
    )
    results = []
    for step_index in range(STEPS):
        query_slot = query_every[step_index]
        key_slot = key_every[step_index]
        value_slot = value_every[step_index]
        moment = cache_length + counts + step_index
        step_query = rotate(query_slot.reshape(slot_count, HEADS, HEAD), moment).astype(
            jnp.bfloat16
        )
        step_key = (
            rotate(key_slot.reshape(slot_count, KV_HEADS, HEAD), moment)
            .astype(jnp.bfloat16)
            .reshape(slot_count, kv_width)
        )
        recent_keys = recent_keys.at[:, step_index].set(step_key)
        recent_values = recent_values.at[:, step_index].set(value_slot)
        recent_live = jnp.broadcast_to(step_indices[None, :] <= step_index, (slot_count, STEPS))
        blocks = (
            (cache_keys, cache_values, cache_live),
            (prompt_keys, prompt_values, prompt_live),
            (recent_keys, recent_values, recent_live),
        )
        results.append(decode_attend(step_query, blocks, scale))
    step_out = jnp.stack(results, axis=0)
    return (prompt_out, step_out)


CHUNKS = 8
MESH = pl.DeviceIdType.MESH
VMEM_LIMIT = 60000 * 1024


def greet(targets):
    barrier = pltpu.get_barrier_semaphore()
    for target in targets:
        pl.semaphore_signal(barrier, inc=1, device_id=target, device_id_type=MESH)
    pl.semaphore_wait(barrier, len(targets))


def project_kernel(
    count, prompt_ref, step_ref, wq_ref, wk_ref, wv_ref,
    pq_ref, pk_ref, pv_ref, sq_ref, sk_ref, sv_ref,
    rows_p, rows_s, vq, vk, vv, acc_q, acc_k, acc_v,
    weight_sem, send_sem, recv_sem,
):
    pool = lax.axis_index("pool")
    me = lax.axis_index("tp")
    f32, bf16 = jnp.float32, jnp.bfloat16
    chips = count // 2
    chip = me // 2
    partner = me + 1 - 2 * lax.rem(me, 2)
    width = prompt_ref.shape[1] // CHUNKS
    fold = width // 4
    bufs = (rows_p, rows_s)
    widths = (width, fold)

    def cols(k, b=0):
        return pl.ds(k * widths[b], widths[b])

    weights = []
    for k in range(CHUNKS):
        for j, (source, target) in enumerate(((wq_ref, vq), (wk_ref, vk), (wv_ref, vv))):
            copy = pltpu.make_async_copy(source.at[cols(k)], target.at[cols(k)], weight_sem.at[j, k])
            weights.append(copy)
    near = ((chip > 0, me - 2), (chip < chips - 1, me + 2))
    barrier = pltpu.get_barrier_semaphore()
    for there, target in near:
        @pl.when(there)
        def _():
            pl.semaphore_signal(barrier, inc=1, device_id=(pool, target), device_id_type=MESH)
    pl.semaphore_signal(barrier, inc=1, device_id=(pool, partner), device_id_type=MESH)
    half = rows_p.shape[1] - prompt_ref.shape[0]
    for k in range(CHUNKS):
        steps = jnp.concatenate([step_ref[i, :, cols(k)].astype(f32) for i in range(STEPS)], axis=0)
        rows_p[me, :, cols(k)] = jnp.concatenate(
            [prompt_ref[:, cols(k)].astype(f32), steps[:half]], axis=0
        ).astype(bf16)
        rows_s[me, :, cols(k, 1)] = jnp.concatenate(
            [steps[half:, j * fold : (j + 1) * fold] for j in range(4)], axis=0
        ).astype(bf16)
    pl.semaphore_wait(barrier, 1 + (chip > 0).astype(jnp.int32) + (chip < chips - 1).astype(jnp.int32))

    def kind(side, distance, handed):
        return 1 + (side * (chips - 1) + distance - 1) * 2 + handed

    def transfer(b, slot, k, which, target):
        place = bufs[b].at[slot, :, cols(k, b)]
        return pltpu.make_async_remote_copy(
            src_ref=place,
            dst_ref=place,
            send_sem=send_sem.at[b, which, k],
            recv_sem=recv_sem.at[b, which, k],
            device_id=(pool, target),
            device_id_type=MESH,
        )

    def send(slot, k, which, target):
        for b in range(2):
            transfer(b, slot, k, which, target).start()

    def arrive(slot, k, which):
        for b in range(2):
            transfer(b, slot, k, which, partner).wait_recv()

    def drain(slot, k, which, target):
        for b in range(2):
            transfer(b, slot, k, which, target).wait_send()

    def source(side, distance):
        if side == 0:
            return chip >= distance, me - 2 * distance
        return chip + distance < chips, me + 2 * distance

    def onward(side):
        return near[1 - side]

    for k in range(CHUNKS):
        for side in range(2):
            there, target = onward(side)
            @pl.when(there)
            def _():
                send(me, k, kind(side, 1, 0), target)
    for k in range(CHUNKS):
        send(me, k, 0, partner)
    for copy in weights:
        copy.start()
    acc_q[...] = jnp.zeros_like(acc_q)
    acc_k[...] = jnp.zeros_like(acc_k)
    acc_v[...] = jnp.zeros_like(acc_v)

    def relay(side, distance, k):
        there, slot = source(side, distance)
        more, target = onward(side)
        @pl.when(there)
        def _():
            arrive(slot, k, kind(side, distance, 0))
            if distance < chips - 1:
                @pl.when(more)
                def _():
                    send(slot, k, kind(side, distance + 1, 0), target)
            send(slot, k, kind(side, distance, 1), partner)

    def multiply(k):
        arrive(partner, k, 0)
        for side in range(2):
            for distance in range(1, chips):
                there, slot = source(side, distance)
                @pl.when(there)
                def _():
                    arrive(slot + partner - me, k, kind(side, distance, 1))
        for j in range(3):
            weights[3 * k + j].wait()
        left_p = rows_p[:, :, cols(k)].reshape(-1, width)
        folded = rows_s[:, :, cols(k, 1)].astype(f32)
        left_s = jnp.concatenate(
            [folded[:, j * half : (j + 1) * half].reshape(-1, fold) for j in range(4)], axis=1
        ).astype(bf16)
        lhs = jnp.concatenate([left_p, left_s], axis=0)
        for vref, acc in ((vq, acc_q), (vk, acc_k), (vv, acc_v)):
            acc[...] += jnp.dot(lhs, vref[cols(k), :], preferred_element_type=f32)

    for distance in range(1, chips):
        for k in range(CHUNKS):
            for side in range(2):
                relay(side, distance, k)
            if distance == chips - 1 and k >= 1:
                multiply(k - 1)
    multiply(CHUNKS - 1)
    split = pq_ref.shape[0]
    tall = rows_p.shape[1]
    for acc, p_ref, s_ref in ((acc_q, pq_ref, sq_ref), (acc_k, pk_ref, sk_ref), (acc_v, pv_ref, sv_ref)):
        p_ref[...] = acc[:split].astype(bf16)
        s_ref[...] = jnp.concatenate(
            [
                piece
                for t in range(count)
                for piece in (
                    acc[(t + 1) * tall - half : (t + 1) * tall],
                    acc[split + t * half : split + (t + 1) * half],
                )
            ],
            axis=0,
        ).astype(bf16)
    for k in range(CHUNKS):
        drain(me, k, 0, partner)
        for side in range(2):
            more, target = onward(side)
            @pl.when(more)
            def _():
                drain(me, k, kind(side, 1, 0), target)
            for distance in range(1, chips):
                there, slot = source(side, distance)
                @pl.when(there)
                def _():
                    drain(slot, k, kind(side, distance, 1), partner)
                    if distance < chips - 1:
                        @pl.when(more)
                        def _():
                            drain(slot, k, kind(side, distance + 1, 0), target)


def gather_project(prompt, step, wq, wk, wv, count):
    depth = prompt.shape[1]
    step_rows = step.shape[0] * step.shape[1]
    half = step_rows // 2
    tall = prompt.shape[0] + half
    widths = (wq.shape[1], wk.shape[1], wv.shape[1])
    anywhere = pl.BlockSpec(memory_space=pl.ANY)
    inside = pl.BlockSpec(memory_space=pltpu.VMEM)
    total = count * (tall + half)
    kinds = 1 + 4 * (count // 2 - 1)
    return pl.pallas_call(
        functools.partial(project_kernel, count),
        out_shape=[jax.ShapeDtypeStruct((count * tall, w), jnp.bfloat16) for w in widths]
        + [jax.ShapeDtypeStruct((count * step_rows, w), jnp.bfloat16) for w in widths],
        in_specs=[inside] * 2 + [anywhere] * 3,
        out_specs=[inside] * 6,
        scratch_shapes=[
            pltpu.VMEM((count, tall, depth), jnp.bfloat16),
            pltpu.VMEM((count, 4 * half, depth // 4), jnp.bfloat16),
        ]
        + [pltpu.VMEM((depth, w), jnp.bfloat16) for w in widths]
        + [pltpu.VMEM((total, w), jnp.float32) for w in widths]
        + [
            pltpu.SemaphoreType.DMA((3, CHUNKS)),
            pltpu.SemaphoreType.DMA((2, kinds, CHUNKS)),
            pltpu.SemaphoreType.DMA((2, kinds, CHUNKS)),
        ],
        compiler_params=pltpu.CompilerParams(
            collective_id=0, has_side_effects=True, vmem_limit_bytes=VMEM_LIMIT
        ),
    )(prompt, step, wq, wk, wv)


def nt(a, b):
    return lax.dot_general(a, b, (((1,), (1,)), ((), ())), preferred_element_type=jnp.float32)


def attend_kernel(
    pools, count, real_rows, scale,
    pq_ref, pk_ref, pv_ref, sq_ref, sk_ref, sv_ref,
    slots_ref, freq_ref, length_ref,
    cache_k_ref, cache_v_ref,
    out_ref, step_out_ref,
    pairs, outgoing, incoming, ck, cv,
    cache_sem, pool_send, pool_recv, tp_send, tp_recv,
):
    pool = lax.axis_index("pool")
    me = lax.axis_index("tp")
    f32, bf16 = jnp.float32, jnp.bfloat16
    heads = pq_ref.shape[1] // HEAD
    caches = [
        pltpu.make_async_copy(cache_k_ref, ck, cache_sem.at[0]),
        pltpu.make_async_copy(cache_v_ref, cv, cache_sem.at[1]),
    ]
    for copy in caches:
        copy.start()
    peers = [lax.rem(pool + d, pools) for d in range(1, pools)]
    mates = [lax.rem(me + d, count) for d in range(1, count)]
    greet([(peer, me) for peer in peers] + [(pool, mate) for mate in mates])
    sign = jnp.where(lax.broadcasted_iota(jnp.int32, (1, HEAD), 1) < HEAD // 2, -1.0, 1.0)
    freq = freq_ref[...]

    def tables(position):
        angles = position.astype(f32) * freq
        return jnp.cos(angles), jnp.sin(angles) * sign

    def turn(values, table):
        return values * table[0] + pltpu.roll(values, HEAD // 2, 1) * table[1]

    rows = pq_ref.shape[0]
    row_at = lax.broadcasted_iota(jnp.int32, (rows, rows), 0)
    col_at = lax.broadcasted_iota(jnp.int32, (rows, rows), 1)
    slot_row = jnp.broadcast_to(slots_ref[pl.ds(pool, 1), :].astype(f32), (8, rows))
    slot_col = jnp.transpose(slot_row)[:, :1]
    allowed = (slot_col == slot_row[:1]) & (col_at <= row_at)
    position = jnp.sum(allowed.astype(f32), axis=1, keepdims=True) - 1.0
    table = tables(position)
    key_rows = turn(pk_ref[...].astype(f32), table).astype(bf16)
    value_rows = pv_ref[...]
    pairs[pool, :, :HEAD] = key_rows
    pairs[pool, :, HEAD:] = value_rows
    sent = []
    for d, peer in enumerate(peers):
        copy = pltpu.make_async_remote_copy(
            src_ref=pairs.at[pool],
            dst_ref=pairs.at[pool],
            send_sem=pool_send.at[d],
            recv_sem=pool_recv.at[d],
            device_id=(peer, me),
            device_id_type=MESH,
        )
        copy.start()
        sent.append(copy)
    blocks = rows // count
    for h in range(heads):
        lanes = slice(h * HEAD, (h + 1) * HEAD)
        query = turn(pq_ref[:, lanes].astype(f32), table).astype(bf16)
        scores = jnp.where(allowed, nt(query, key_rows) * scale, negative_fill)
        raised = jnp.exp(scores - jnp.max(scores, axis=1, keepdims=True))
        weights = (raised / jnp.sum(raised, axis=1, keepdims=True)).astype(bf16)
        context = jnp.dot(weights, value_rows, preferred_element_type=f32).astype(bf16)
        for t in range(count):
            out_ref[t * real_rows : (t + 1) * real_rows, lanes] = context[
                t * blocks : t * blocks + real_rows
            ]
    step_rows = sq_ref.shape[0]
    block = step_rows // count
    local = block // STEPS
    first = pool * count * local

    def row_slot(index):
        return first + (index // block) * local + lax.rem(index, local)

    def row_step(index):
        return lax.rem(index, block) // local

    index_col = lax.broadcasted_iota(jnp.int32, (step_rows, 1), 0)
    index_row = lax.broadcasted_iota(jnp.int32, (1, step_rows), 1)
    all_slots = jnp.concatenate([slots_ref[p : p + 1, :] for p in range(pools)], axis=1)
    match = all_slots == row_slot(index_col)
    tally = jnp.sum(match.astype(f32), axis=1, keepdims=True)
    named = tally > 0.0
    moment = jnp.where(named, tally + row_step(index_col).astype(f32), 0.0)
    step_table = tables(moment)
    step_key = turn(sk_ref[...].astype(f32), step_table)
    step_value = sv_ref[...]
    step_key_rows = step_key.astype(bf16)
    recent = (row_slot(index_col) == row_slot(index_row)) & (
        row_step(index_row) <= row_step(index_col)
    )
    for d in range(1, pools):
        source = lax.rem(pool + pools - d, pools)
        pltpu.make_async_remote_copy(
            src_ref=pairs.at[source],
            dst_ref=pairs.at[source],
            send_sem=pool_send.at[d - 1],
            recv_sem=pool_recv.at[d - 1],
            device_id=(peers[d - 1], me),
            device_id_type=MESH,
        ).wait_recv()
    prompt_keys = pairs[:, :, :HEAD].reshape(-1, HEAD)
    prompt_values = pairs[:, :, HEAD:].reshape(-1, HEAD)

    def pack(lanes, values):
        outgoing[:, :, lanes] = values.reshape(count, block, HEAD).astype(bf16)

    for h in range(heads):
        lanes = slice(h * HEAD, (h + 1) * HEAD)
        turned = turn(sq_ref[:, lanes].astype(f32), step_table)
        query = turned.astype(bf16)
        far = jnp.where(match, nt(query, prompt_keys) * scale, negative_fill)
        near = jnp.where(recent, nt(query, step_key_rows) * scale, negative_fill)
        peak = jnp.maximum(
            jnp.max(far, axis=1, keepdims=True), jnp.max(near, axis=1, keepdims=True)
        )
        far, near = jnp.exp(far - peak), jnp.exp(near - peak)
        bottom = jnp.sum(far, axis=1, keepdims=True) + jnp.sum(near, axis=1, keepdims=True)
        context = jnp.dot(
            (far / bottom).astype(bf16), prompt_values, preferred_element_type=f32
        ) + jnp.dot((near / bottom).astype(bf16), step_value, preferred_element_type=f32)
        pack(lanes, jnp.where(named, context, turned))
    wide = heads * HEAD
    pack(slice(wide, wide + HEAD), step_key)
    pack(slice(wide + HEAD, wide + 2 * HEAD), step_value.astype(f32))
    for d, mate in enumerate(mates):
        copy = pltpu.make_async_remote_copy(
            src_ref=outgoing.at[mate],
            dst_ref=incoming.at[me],
            send_sem=tp_send.at[d],
            recv_sem=tp_recv.at[d],
            device_id=(pool, mate),
            device_id_type=MESH,
        )
        copy.start()
        sent.append(copy)
    incoming[me] = outgoing[me]
    own_col = lax.broadcasted_iota(jnp.int32, (block, 1), 0)
    own_slot = first + me * local + lax.rem(own_col, local)
    own_named = jnp.sum((all_slots == own_slot).astype(f32), axis=1, keepdims=True) > 0.0
    lengths = jnp.zeros((block, 1), jnp.int32)
    for s in range(local):
        lengths = jnp.where(lax.rem(own_col, local) == s, length_ref[s], lengths)
    own_table = tables((lengths + own_col // local).astype(f32))
    many = heads * block
    many_col = lax.rem(lax.broadcasted_iota(jnp.int32, (many, 1), 0), block)
    block_row = lax.broadcasted_iota(jnp.int32, (1, block), 1)
    own_recent = (lax.rem(many_col, local) == lax.rem(block_row, local)) & (
        block_row // local <= many_col // local
    )
    many_lengths = jnp.concatenate([lengths] * heads, axis=0)
    extent = ck.shape[1]
    cache_at = lax.broadcasted_iota(jnp.int32, (1, extent), 1)
    live = [
        cache_at < jnp.where(lax.rem(many_col, local) == s, many_lengths, 0) for s in range(local)
    ]
    for copy in caches:
        copy.wait()
    for d in range(1, count):
        source = lax.rem(me + count - d, count)
        pltpu.make_async_remote_copy(
            src_ref=outgoing.at[source],
            dst_ref=incoming.at[source],
            send_sem=tp_send.at[d - 1],
            recv_sem=tp_recv.at[d - 1],
            device_id=(pool, mates[d - 1]),
            device_id_type=MESH,
        ).wait_recv()
    for t in range(count):
        got = incoming[t].astype(f32)
        query = jnp.concatenate(
            [turn(got[:, h * HEAD : (h + 1) * HEAD], own_table) for h in range(heads)], axis=0
        ).astype(bf16)
        key = turn(got[:, wide : wide + HEAD], own_table).astype(bf16)
        value = got[:, wide + HEAD :].astype(bf16)
        lanes = slice(t * HEAD, (t + 1) * HEAD)
        parts = [
            jnp.where(live[s], nt(query, ck[s, :, lanes]) * scale, negative_fill)
            for s in range(local)
        ]
        parts.append(jnp.where(own_recent, nt(query, key) * scale, negative_fill))
        peak = functools.reduce(
            jnp.maximum, [jnp.max(part, axis=1, keepdims=True) for part in parts]
        )
        parts = [jnp.exp(part - peak) for part in parts]
        bottom = sum(jnp.sum(part, axis=1, keepdims=True) for part in parts)
        shares = [(part / bottom).astype(bf16) for part in parts]
        context = jnp.dot(shares[-1], value, preferred_element_type=f32)
        for s in range(local):
            context = context + jnp.dot(
                shares[s], cv[s, :, lanes], preferred_element_type=f32
            )
        for h in range(heads):
            at = slice((t * heads + h) * HEAD, (t * heads + h + 1) * HEAD)
            chosen = jnp.where(
                own_named,
                got[:, h * HEAD : (h + 1) * HEAD],
                context[h * block : (h + 1) * block],
            ).astype(bf16)
            for i in range(STEPS):
                step_out_ref[i, :, at] = chosen[i * local : (i + 1) * local]
    for copy in sent:
        copy.wait_send()


def fast_device(
    pools, prompt_states, stretch_slot, cache_length, cache_keys, cache_values, step_states,
    query_weight, key_weight, value_weight,
):
    count = lax.axis_size("tp")
    pool = lax.axis_index("pool")
    real_rows = prompt_states.shape[0]
    local = cache_length.shape[0]
    padded = real_rows + STEPS * local // 2
    projected = gather_project(
        prompt_states, step_states, query_weight, key_weight, value_weight, count
    )
    slots = jnp.pad(
        stretch_slot.reshape(pools, count, real_rows),
        ((0, 0), (0, 0), (0, padded - real_rows)),
        constant_values=-1,
    ).reshape(pools, count * padded)
    half = frequencies(HEAD // 2)
    freq = jnp.concatenate([half, half])[None, :]
    inside = pl.BlockSpec(memory_space=pltpu.VMEM)
    anywhere = pl.BlockSpec(memory_space=pl.ANY)
    width = query_weight.shape[1]
    block = STEPS * local
    prompt_out, step_out = pl.pallas_call(
        functools.partial(attend_kernel, pools, count, real_rows, 1.0 / math.sqrt(HEAD)),
        out_shape=[
            jax.ShapeDtypeStruct((count * real_rows, width), jnp.bfloat16),
            jax.ShapeDtypeStruct((STEPS, local, count * width), jnp.bfloat16),
        ],
        in_specs=[inside] * 8 + [pl.BlockSpec(memory_space=pltpu.SMEM)] + [anywhere] * 2,
        out_specs=[inside] * 2,
        scratch_shapes=[
            pltpu.VMEM((pools, count * padded, 2 * HEAD), jnp.bfloat16),
            pltpu.VMEM((count, block, width + 2 * HEAD), jnp.bfloat16),
            pltpu.VMEM((count, block, width + 2 * HEAD), jnp.bfloat16),
            pltpu.VMEM(cache_keys.shape, jnp.bfloat16),
            pltpu.VMEM(cache_values.shape, jnp.bfloat16),
            pltpu.SemaphoreType.DMA((2,)),
            pltpu.SemaphoreType.DMA((pools - 1,)),
            pltpu.SemaphoreType.DMA((pools - 1,)),
            pltpu.SemaphoreType.DMA((count - 1,)),
            pltpu.SemaphoreType.DMA((count - 1,)),
        ],
        compiler_params=pltpu.CompilerParams(
            collective_id=1, has_side_effects=True, vmem_limit_bytes=VMEM_LIMIT
        ),
    )(
        *projected, slots, freq, cache_length, cache_keys, cache_values,
    )
    return prompt_out, step_out


def per_device(pools, *args):
    count = lax.axis_size("tp")
    extra = args[2].shape[0] * STEPS // 2
    if count == KV_HEADS and args[7].shape[1] == HEAD and extra == 4 and (args[0].shape[0] + extra) % 16 == 0:
        return fast_device(pools, *args)
    return on_device(*args)


def solution(mesh):
    in_specs = (
        P(("pool", "tp"), None),
        P(),
        P(("pool", "tp")),
        P(("pool", "tp"), None, None),
        P(("pool", "tp"), None, None),
        P(None, ("pool", "tp"), None),
        P(None, "tp"),
        P(None, "tp"),
        P(None, "tp"),
    )
    out_specs = (P("pool", "tp"), P(None, ("pool", "tp"), None))
    return jax.shard_map(
        functools.partial(per_device, mesh.shape["pool"]), mesh=mesh, in_specs=in_specs, out_specs=out_specs, check_vma=False
    )
```

```python
import functools
import math

import jax
import jax.numpy as jnp
from jax import lax
from jax.experimental import pallas as pl
from jax.experimental.pallas import tpu as pltpu
from jax.sharding import PartitionSpec as P

HEADS = 64
KV_HEADS = 8
HEAD = 128
PMAX = 32
STEPS = 4


rope_base = 500000.0
negative_fill = -1e30


def frequencies(half):
    indices = jnp.arange(half, dtype=jnp.float32)
    inverse = rope_base ** (-2.0 * indices / (2.0 * half))
    wavelength = 2.0 * math.pi / inverse
    blend = (8192.0 / wavelength - 1.0) / 3.0
    middle = (1.0 - blend) * inverse / 8.0 + blend * inverse
    scaled = jnp.where(wavelength > 8192.0, inverse / 8.0, inverse)
    inside = (wavelength >= 2048.0) & (wavelength <= 8192.0)
    return jnp.where(inside, middle, scaled)


def rotate(values, positions):
    half = values.shape[-1] // 2
    angles = positions.astype(jnp.float32)[..., None, None] * frequencies(half)
    cosine = jnp.cos(angles)
    sine = jnp.sin(angles)
    upper = values[..., :half].astype(jnp.float32)
    lower = values[..., half:].astype(jnp.float32)
    return jnp.concatenate([upper * cosine - lower * sine, lower * cosine + upper * sine], axis=-1)


def run_positions(slots, span):
    indices = jnp.arange(slots.shape[0], dtype=jnp.int32)
    previous = jnp.concatenate([slots[:1] - 1, slots[:-1]])
    opening = (slots != previous) | (indices % span == 0)
    starts = lax.cummax(jnp.where(opening, indices, 0), axis=0)
    return indices - starts


def normalize(scores):
    peak = jnp.max(scores, axis=-1, keepdims=True)
    raised = jnp.exp(scores - peak)
    return (raised / jnp.sum(raised, axis=-1, keepdims=True)).astype(jnp.bfloat16)


def project(states, query_weight, key_weight, value_weight):
    products = [
        jnp.dot(states, weight, preferred_element_type=jnp.float32)
        for weight in (query_weight, key_weight, value_weight)
    ]
    return jnp.concatenate(products, axis=1).astype(jnp.bfloat16)


def decode_attend(queries, blocks, scale):
    slot_count = queries.shape[0]
    grouped = queries.reshape(slot_count, KV_HEADS, HEADS // KV_HEADS, HEAD)
    score_blocks = []
    for key_block, value_block, live_rows in blocks:
        key_heads = key_block.reshape(slot_count, key_block.shape[1], KV_HEADS, HEAD)
        scores = (
            jnp.einsum("rkgd,rlkd->rkgl", grouped, key_heads, preferred_element_type=jnp.float32)
            * scale
        )
        score_blocks.append(jnp.where(live_rows[:, None, None, :], scores, negative_fill))
    weights = normalize(jnp.concatenate(score_blocks, axis=-1))
    context = jnp.zeros((slot_count, KV_HEADS, HEADS // KV_HEADS, HEAD), jnp.float32)
    position = 0
    for key_block, value_block, live_rows in blocks:
        extent = value_block.shape[1]
        shares = weights[..., position : position + extent]
        value_heads = value_block.reshape(slot_count, extent, KV_HEADS, HEAD)
        context = context + jnp.einsum(
            "rkgl,rlkd->rkgd", shares, value_heads, preferred_element_type=jnp.float32
        )
        position = position + extent
    return context.reshape(slot_count, HEADS * HEAD).astype(jnp.bfloat16)


def on_device(
    prompt_states,
    stretch_slot,
    cache_length,
    cache_keys,
    cache_values,
    step_states,
    query_weight,
    key_weight,
    value_weight,
):
    pool_index = lax.axis_index("pool")
    tp_index = lax.axis_index("tp")
    tp_count = lax.axis_size("tp")
    query_width = query_weight.shape[1]
    column_width = key_weight.shape[1]
    kv_width = KV_HEADS * HEAD
    local_heads = query_width // HEAD
    group_size = HEADS // KV_HEADS
    scale = 1.0 / math.sqrt(HEAD)
    projected = project(
        lax.all_gather(prompt_states, "tp", axis=0, tiled=True),
        query_weight,
        key_weight,
        value_weight,
    )
    stretch_rows = projected.shape[0]
    query_raw = projected[:, :query_width]
    key_part = projected[:, query_width : query_width + column_width]
    value_part = projected[:, query_width + column_width :]
    key_raw, value_rows = (
        lax.all_gather(key_part, "tp", axis=1, tiled=True),
        lax.all_gather(value_part, "tp", axis=1, tiled=True),
    )
    group_slots = lax.dynamic_slice_in_dim(stretch_slot, pool_index * stretch_rows, stretch_rows, 0)
    positions = run_positions(group_slots, stretch_rows)
    queries = rotate(query_raw.reshape(stretch_rows, local_heads, HEAD), positions).astype(
        jnp.bfloat16
    )
    key_rows = rotate(key_raw.reshape(stretch_rows, KV_HEADS, HEAD), positions).astype(jnp.bfloat16)
    kv_index = tp_index * local_heads // group_size
    key_head = lax.dynamic_index_in_dim(key_rows, kv_index, 1, keepdims=False)
    value_head = lax.dynamic_index_in_dim(
        value_rows.reshape(stretch_rows, KV_HEADS, HEAD), kv_index, 1, keepdims=False
    )
    scores = (
        jnp.einsum("qhd,ld->hql", queries, key_head, preferred_element_type=jnp.float32) * scale
    )
    indices = jnp.arange(stretch_rows, dtype=jnp.int32)
    allowed = (group_slots[:, None] == group_slots[None, :]) & (
        indices[None, :] <= indices[:, None]
    )
    weights = normalize(jnp.where(allowed[None], scores, negative_fill))
    context = jnp.einsum("hql,ld->qhd", weights, value_head, preferred_element_type=jnp.float32)
    prompt_out = context.reshape(stretch_rows, query_width).astype(jnp.bfloat16)
    kv_pair = jnp.concatenate([key_rows.reshape(stretch_rows, kv_width), value_rows], axis=1)
    slot_count = cache_length.shape[0]
    device_index = pool_index * tp_count + tp_index
    my_slots = device_index * slot_count + jnp.arange(slot_count, dtype=jnp.int32)
    all_rows = stretch_slot.shape[0]
    all_indices = jnp.arange(all_rows, dtype=jnp.int32)
    matches = stretch_slot[None, :] == my_slots[:, None]
    counts = jnp.sum(matches, axis=1)
    offsets = jnp.arange(PMAX, dtype=jnp.int32)
    everything = lax.all_gather(kv_pair, "pool", axis=0, tiled=True)
    begins = jnp.min(jnp.where(matches, all_indices[None, :], all_rows), axis=1)
    row_ids = jnp.clip(begins[:, None] + offsets[None, :], 0, all_rows - 1)
    prompt_pair = jnp.take(everything, row_ids.reshape(-1), axis=0).reshape(
        slot_count, PMAX, 2 * kv_width
    )
    prompt_keys = prompt_pair[:, :, :kv_width]
    prompt_values = prompt_pair[:, :, kv_width:]
    recent_keys = jnp.zeros((slot_count, STEPS, kv_width), jnp.bfloat16)
    recent_values = jnp.zeros((slot_count, STEPS, kv_width), jnp.bfloat16)
    cache_live = jnp.arange(cache_keys.shape[1], dtype=jnp.int32)[None, :] < cache_length[:, None]
    prompt_live = offsets[None, :] < counts[:, None]
    step_indices = jnp.arange(STEPS, dtype=jnp.int32)
    section = lax.all_gather(step_states, "tp", axis=1, tiled=True)
    step_count = section.shape[0]
    row_count = section.shape[1]
    flat = project(
        section.reshape(step_count * row_count, section.shape[2]),
        query_weight,
        key_weight,
        value_weight,
    )
    every_projected = flat.reshape(step_count, row_count, flat.shape[1])
    query_every, key_every, value_every = (
        lax.all_to_all(
            every_projected[:, :, :query_width], "tp", split_axis=1, concat_axis=2, tiled=True
        ),
        lax.all_to_all(
            every_projected[:, :, query_width : query_width + column_width],
            "tp",
            split_axis=1,
            concat_axis=2,
            tiled=True,
        ),
        lax.all_to_all(
            every_projected[:, :, query_width + column_width :],
            "tp",
            split_axis=1,
            concat_axis=2,
            tiled=True,
        ),
    )
    results = []
    for step_index in range(STEPS):
        query_slot = query_every[step_index]
        key_slot = key_every[step_index]
        value_slot = value_every[step_index]
        moment = cache_length + counts + step_index
        step_query = rotate(query_slot.reshape(slot_count, HEADS, HEAD), moment).astype(
            jnp.bfloat16
        )
        step_key = (
            rotate(key_slot.reshape(slot_count, KV_HEADS, HEAD), moment)
            .astype(jnp.bfloat16)
            .reshape(slot_count, kv_width)
        )
        recent_keys = recent_keys.at[:, step_index].set(step_key)
        recent_values = recent_values.at[:, step_index].set(value_slot)
        recent_live = jnp.broadcast_to(step_indices[None, :] <= step_index, (slot_count, STEPS))
        blocks = (
            (cache_keys, cache_values, cache_live),
            (prompt_keys, prompt_values, prompt_live),
            (recent_keys, recent_values, recent_live),
        )
        results.append(decode_attend(step_query, blocks, scale))
    step_out = jnp.stack(results, axis=0)
    return (prompt_out, step_out)


CHUNKS = 8
MESH = pl.DeviceIdType.MESH
VMEM_LIMIT = 60000 * 1024


def project_kernel(
    pools, count, prepare, prompt_ref, step_ref, wq_ref, wk_ref, wv_ref,
    pq_ref, pk_ref, pv_ref, sq_ref, sk_ref, sv_ref,
    rows_p, rows_s, vq, vk, vv, acc_q, acc_k, acc_v,
    weight_sem, send_sem, recv_sem,
):
    pool = lax.axis_index("pool")
    me = lax.axis_index("tp")
    f32, bf16 = jnp.float32, jnp.bfloat16
    chips = count // 2
    chip = me // 2
    partner = me + 1 - 2 * lax.rem(me, 2)
    width = prompt_ref.shape[1] // CHUNKS
    fold = width // 4
    bufs = (rows_p, rows_s)
    widths = (width, fold)

    def cols(k, b=0):
        return pl.ds(k * widths[b], widths[b])

    weights = []
    for k in range(CHUNKS):
        for j, (source, target) in enumerate(((wq_ref, vq), (wk_ref, vk), (wv_ref, vv))):
            copy = pltpu.make_async_copy(source.at[cols(k)], target.at[cols(k)], weight_sem.at[j, k])
            weights.append(copy)
    near = ((chip > 0, me - 2), (chip < chips - 1, me + 2))
    barrier = pltpu.get_barrier_semaphore()
    for d in range(1, pools):
        target = (lax.rem(pool + d, pools), me)
        pl.semaphore_signal(barrier, inc=1, device_id=target, device_id_type=MESH)
    for d in range(1, count):
        target = (pool, lax.rem(me + d, count))
        pl.semaphore_signal(barrier, inc=1, device_id=target, device_id_type=MESH)
    half = rows_p.shape[1] - prompt_ref.shape[0]
    for k in range(CHUNKS):
        steps = jnp.concatenate([step_ref[i, :, cols(k)].astype(f32) for i in range(STEPS)], axis=0)
        rows_p[me, :, cols(k)] = jnp.concatenate(
            [prompt_ref[:, cols(k)].astype(f32), steps[:half]], axis=0
        ).astype(bf16)
        rows_s[me, :, cols(k, 1)] = jnp.concatenate(
            [steps[half:, j * fold : (j + 1) * fold] for j in range(4)], axis=0
        ).astype(bf16)
    pl.semaphore_wait(barrier, pools + count - 2)

    def kind(side, distance, handed):
        return 1 + (side * (chips - 1) + distance - 1) * 2 + handed

    def transfer(b, slot, k, which, target):
        place = bufs[b].at[slot, :, cols(k, b)]
        return pltpu.make_async_remote_copy(
            src_ref=place,
            dst_ref=place,
            send_sem=send_sem.at[b, which, k],
            recv_sem=recv_sem.at[b, which, k],
            device_id=(pool, target),
            device_id_type=MESH,
        )

    def send(slot, k, which, target):
        for b in range(2):
            transfer(b, slot, k, which, target).start()

    def arrive(slot, k, which):
        for b in range(2):
            transfer(b, slot, k, which, partner).wait_recv()

    def drain(slot, k, which, target):
        for b in range(2):
            transfer(b, slot, k, which, target).wait_send()

    def source(side, distance):
        if side == 0:
            return chip >= distance, me - 2 * distance
        return chip + distance < chips, me + 2 * distance

    def onward(side):
        return near[1 - side]

    for k in range(CHUNKS):
        for side in range(2):
            there, target = onward(side)
            @pl.when(there)
            def _():
                send(me, k, kind(side, 1, 0), target)
    for k in range(CHUNKS):
        send(me, k, 0, partner)
    for copy in weights:
        copy.start()
    prepare()
    acc_q[...] = jnp.zeros_like(acc_q)
    acc_k[...] = jnp.zeros_like(acc_k)
    acc_v[...] = jnp.zeros_like(acc_v)

    def relay(side, distance, k):
        there, slot = source(side, distance)
        more, target = onward(side)
        @pl.when(there)
        def _():
            arrive(slot, k, kind(side, distance, 0))
            if distance < chips - 1:
                @pl.when(more)
                def _():
                    send(slot, k, kind(side, distance + 1, 0), target)
            send(slot, k, kind(side, distance, 1), partner)

    def multiply(k):
        arrive(partner, k, 0)
        for side in range(2):
            for distance in range(1, chips):
                there, slot = source(side, distance)
                @pl.when(there)
                def _():
                    arrive(slot + partner - me, k, kind(side, distance, 1))
        for j in range(3):
            weights[3 * k + j].wait()
        left_p = rows_p[:, :, cols(k)].reshape(-1, width)
        folded = rows_s[:, :, cols(k, 1)].astype(f32)
        left_s = jnp.concatenate(
            [folded[:, j * half : (j + 1) * half].reshape(-1, fold) for j in range(4)], axis=1
        ).astype(bf16)
        lhs = jnp.concatenate([left_p, left_s], axis=0)
        for vref, acc in ((vq, acc_q), (vk, acc_k), (vv, acc_v)):
            acc[...] += jnp.dot(lhs, vref[cols(k), :], preferred_element_type=f32)

    for distance in range(1, chips):
        for k in range(CHUNKS):
            for side in range(2):
                relay(side, distance, k)
            if distance == chips - 1 and k >= 1:
                multiply(k - 1)
    multiply(CHUNKS - 1)
    split = pq_ref.shape[0]
    tall = rows_p.shape[1]
    for acc, p_ref, s_ref in ((acc_q, pq_ref, sq_ref), (acc_k, pk_ref, sk_ref), (acc_v, pv_ref, sv_ref)):
        p_ref[...] = acc[:split].astype(bf16)
        s_ref[...] = jnp.concatenate(
            [
                piece
                for t in range(count)
                for piece in (
                    acc[(t + 1) * tall - half : (t + 1) * tall],
                    acc[split + t * half : split + (t + 1) * half],
                )
            ],
            axis=0,
        ).astype(bf16)
    for k in range(CHUNKS):
        drain(me, k, 0, partner)
        for side in range(2):
            more, target = onward(side)
            @pl.when(more)
            def _():
                drain(me, k, kind(side, 1, 0), target)
            for distance in range(1, chips):
                there, slot = source(side, distance)
                @pl.when(there)
                def _():
                    drain(slot, k, kind(side, distance, 1), partner)
                    if distance < chips - 1:
                        @pl.when(more)
                        def _():
                            drain(slot, k, kind(side, distance + 1, 0), target)


def nt(a, b):
    return lax.dot_general(a, b, (((1,), (1,)), ((), ())), preferred_element_type=jnp.float32)


def whole_kernel(
    pools, count, real_rows, scale,
    prompt_ref, step_ref, wq_ref, wk_ref, wv_ref,
    slots_ref, freq_ref, length_ref, cache_k_ref, cache_v_ref,
    out_hbm, step_out_hbm,
    pq_ref, pk_ref, pv_ref, sq_ref, sk_ref, sv_ref,
    rows_p, rows_s, vq, vk, vv, acc_q, acc_k, acc_v,
    out_ref, step_out_ref, prompt_table, step_table_ref, own_table_ref,
    pairs, outgoing, incoming, ck, cv,
    weight_sem, send_sem, recv_sem,
    cache_sem, out_sem, pool_send, pool_recv, tp_send, tp_recv,
):
    pool = lax.axis_index("pool")
    me = lax.axis_index("tp")
    f32, bf16 = jnp.float32, jnp.bfloat16
    heads = pq_ref.shape[1] // HEAD
    rows = pq_ref.shape[0]
    step_rows = sq_ref.shape[0]
    block = step_rows // count
    local = block // STEPS
    first = pool * count * local
    caches = [
        pltpu.make_async_copy(cache_k_ref, ck, cache_sem.at[0]),
        pltpu.make_async_copy(cache_v_ref, cv, cache_sem.at[1]),
    ]
    peers = [lax.rem(pool + d, pools) for d in range(1, pools)]
    mates = [lax.rem(me + d, count) for d in range(1, count)]
    sign = jnp.where(lax.broadcasted_iota(jnp.int32, (1, HEAD), 1) < HEAD // 2, -1.0, 1.0)

    def keep(position, table_ref):
        angles = position.astype(f32) * freq_ref[...]
        table_ref[0] = jnp.cos(angles)
        table_ref[1] = jnp.sin(angles) * sign

    def turn(values, table):
        return values * table[0] + pltpu.roll(values, HEAD // 2, 1) * table[1]

    def row_slot(index):
        return first + (index // block) * local + lax.rem(index, local)

    def row_step(index):
        return lax.rem(index, block) // local

    def prompt_mask():
        row_at = lax.broadcasted_iota(jnp.int32, (rows, rows), 0)
        col_at = lax.broadcasted_iota(jnp.int32, (rows, rows), 1)
        slot_row = jnp.broadcast_to(slots_ref[pl.ds(pool, 1), :].astype(f32), (8, rows))
        slot_col = jnp.transpose(slot_row)[:, :1]
        return (slot_col == slot_row[:1]) & (col_at <= row_at)

    def every_slot():
        return jnp.concatenate([slots_ref[p : p + 1, :] for p in range(pools)], axis=1)

    index_col = lax.broadcasted_iota(jnp.int32, (step_rows, 1), 0)
    index_row = lax.broadcasted_iota(jnp.int32, (1, step_rows), 1)
    own_col = lax.broadcasted_iota(jnp.int32, (block, 1), 0)

    def own_lengths():
        lengths = jnp.zeros((block, 1), jnp.int32)
        for s in range(local):
            lengths = jnp.where(lax.rem(own_col, local) == s, length_ref[s], lengths)
        return lengths

    def tallies():
        match = every_slot() == row_slot(index_col)
        return match, jnp.sum(match.astype(f32), axis=1, keepdims=True)

    def prepare():
        for copy in caches:
            copy.start()
        keep(jnp.sum(prompt_mask().astype(f32), axis=1, keepdims=True) - 1.0, prompt_table)
        tally = tallies()[1]
        keep(jnp.where(tally > 0.0, tally + row_step(index_col).astype(f32), 0.0), step_table_ref)
        keep(own_lengths() + own_col // local, own_table_ref)

    project_kernel(
        pools, count, prepare, prompt_ref, step_ref, wq_ref, wk_ref, wv_ref,
        pq_ref, pk_ref, pv_ref, sq_ref, sk_ref, sv_ref,
        rows_p, rows_s, vq, vk, vv, acc_q, acc_k, acc_v,
        weight_sem, send_sem, recv_sem,
    )
    allowed = prompt_mask()
    table = prompt_table[0], prompt_table[1]
    key_rows = turn(pk_ref[...].astype(f32), table).astype(bf16)
    value_rows = pv_ref[...]
    pairs[pool, :, :HEAD] = key_rows
    pairs[pool, :, HEAD:] = value_rows
    sent = []
    for d, peer in enumerate(peers):
        copy = pltpu.make_async_remote_copy(
            src_ref=pairs.at[pool],
            dst_ref=pairs.at[pool],
            send_sem=pool_send.at[d],
            recv_sem=pool_recv.at[d],
            device_id=(peer, me),
            device_id_type=MESH,
        )
        copy.start()
        sent.append(copy)
    blocks = rows // count
    stores = []

    def prompt_head(h):
        lanes = slice(h * HEAD, (h + 1) * HEAD)
        query = turn(pq_ref[:, lanes].astype(f32), table).astype(bf16)
        scores = jnp.where(allowed, nt(query, key_rows) * scale, negative_fill)
        raised = jnp.exp(scores - jnp.max(scores, axis=1, keepdims=True))
        weights = (raised / jnp.sum(raised, axis=1, keepdims=True)).astype(bf16)
        context = jnp.dot(weights, value_rows, preferred_element_type=f32).astype(bf16)
        for t in range(count):
            out_ref[t * real_rows : (t + 1) * real_rows, lanes] = context[
                t * blocks : t * blocks + real_rows
            ]
        copy = pltpu.make_async_copy(out_ref.at[:, lanes], out_hbm.at[:, lanes], out_sem.at[h])
        copy.start()
        stores.append(copy)

    for h in range(heads // 2):
        prompt_head(h)
    match, tally = tallies()
    named = tally > 0.0
    step_table = step_table_ref[0], step_table_ref[1]
    step_key = turn(sk_ref[...].astype(f32), step_table)
    step_value = sv_ref[...]
    step_key_rows = step_key.astype(bf16)
    recent = (row_slot(index_col) == row_slot(index_row)) & (
        row_step(index_row) <= row_step(index_col)
    )
    for d in range(1, pools):
        source = lax.rem(pool + pools - d, pools)
        pltpu.make_async_remote_copy(
            src_ref=pairs.at[source],
            dst_ref=pairs.at[source],
            send_sem=pool_send.at[d - 1],
            recv_sem=pool_recv.at[d - 1],
            device_id=(peers[d - 1], me),
            device_id_type=MESH,
        ).wait_recv()
    prompt_keys = pairs[:, :, :HEAD].reshape(-1, HEAD)
    prompt_values = pairs[:, :, HEAD:].reshape(-1, HEAD)

    def pack(lanes, values):
        outgoing[:, :, lanes] = values.reshape(count, block, HEAD).astype(bf16)

    for h in range(heads):
        lanes = slice(h * HEAD, (h + 1) * HEAD)
        turned = turn(sq_ref[:, lanes].astype(f32), step_table)
        query = turned.astype(bf16)
        far = jnp.where(match, nt(query, prompt_keys) * scale, negative_fill)
        near = jnp.where(recent, nt(query, step_key_rows) * scale, negative_fill)
        peak = jnp.maximum(
            jnp.max(far, axis=1, keepdims=True), jnp.max(near, axis=1, keepdims=True)
        )
        far, near = jnp.exp(far - peak), jnp.exp(near - peak)
        bottom = jnp.sum(far, axis=1, keepdims=True) + jnp.sum(near, axis=1, keepdims=True)
        context = jnp.dot(
            (far / bottom).astype(bf16), prompt_values, preferred_element_type=f32
        ) + jnp.dot((near / bottom).astype(bf16), step_value, preferred_element_type=f32)
        pack(lanes, jnp.where(named, context, turned))
    wide = heads * HEAD
    pack(slice(wide, wide + HEAD), step_key)
    pack(slice(wide + HEAD, wide + 2 * HEAD), step_value.astype(f32))
    for d, mate in enumerate(mates):
        copy = pltpu.make_async_remote_copy(
            src_ref=outgoing.at[mate],
            dst_ref=incoming.at[me],
            send_sem=tp_send.at[d],
            recv_sem=tp_recv.at[d],
            device_id=(pool, mate),
            device_id_type=MESH,
        )
        copy.start()
        sent.append(copy)
    incoming[me] = outgoing[me]
    for h in range(heads // 2, heads):
        prompt_head(h)
    own_slot = first + me * local + lax.rem(own_col, local)
    own_named = jnp.sum((every_slot() == own_slot).astype(f32), axis=1, keepdims=True) > 0.0
    lengths = own_lengths()
    own_table = own_table_ref[0], own_table_ref[1]
    many = heads * block
    many_col = lax.rem(lax.broadcasted_iota(jnp.int32, (many, 1), 0), block)
    block_row = lax.broadcasted_iota(jnp.int32, (1, block), 1)
    own_recent = (lax.rem(many_col, local) == lax.rem(block_row, local)) & (
        block_row // local <= many_col // local
    )
    many_lengths = jnp.concatenate([lengths] * heads, axis=0)
    extent = ck.shape[1]
    cache_at = lax.broadcasted_iota(jnp.int32, (1, extent), 1)
    live = [
        cache_at < jnp.where(lax.rem(many_col, local) == s, many_lengths, 0) for s in range(local)
    ]
    for copy in caches:
        copy.wait()
    for d in range(1, count):
        source = lax.rem(me + count - d, count)
        pltpu.make_async_remote_copy(
            src_ref=outgoing.at[source],
            dst_ref=incoming.at[source],
            send_sem=tp_send.at[d - 1],
            recv_sem=tp_recv.at[d - 1],
            device_id=(pool, mates[d - 1]),
            device_id_type=MESH,
        ).wait_recv()
    for t in range(count):
        got = incoming[t].astype(f32)
        query = jnp.concatenate(
            [turn(got[:, h * HEAD : (h + 1) * HEAD], own_table) for h in range(heads)], axis=0
        ).astype(bf16)
        key = turn(got[:, wide : wide + HEAD], own_table).astype(bf16)
        value = got[:, wide + HEAD :].astype(bf16)
        lanes = slice(t * HEAD, (t + 1) * HEAD)
        parts = [
            jnp.where(live[s], nt(query, ck[s, :, lanes]) * scale, negative_fill)
            for s in range(local)
        ]
        parts.append(jnp.where(own_recent, nt(query, key) * scale, negative_fill))
        peak = functools.reduce(
            jnp.maximum, [jnp.max(part, axis=1, keepdims=True) for part in parts]
        )
        parts = [jnp.exp(part - peak) for part in parts]
        bottom = sum(jnp.sum(part, axis=1, keepdims=True) for part in parts)
        shares = [(part / bottom).astype(bf16) for part in parts]
        context = jnp.dot(shares[-1], value, preferred_element_type=f32)
        for s in range(local):
            context = context + jnp.dot(
                shares[s], cv[s, :, lanes], preferred_element_type=f32
            )
        for h in range(heads):
            at = slice((t * heads + h) * HEAD, (t * heads + h + 1) * HEAD)
            chosen = jnp.where(
                own_named,
                got[:, h * HEAD : (h + 1) * HEAD],
                context[h * block : (h + 1) * block],
            ).astype(bf16)
            for i in range(STEPS):
                step_out_ref[i, :, at] = chosen[i * local : (i + 1) * local]
        span = slice(t * wide, (t + 1) * wide)
        copy = pltpu.make_async_copy(
            step_out_ref.at[:, :, span], step_out_hbm.at[:, :, span], out_sem.at[heads + t]
        )
        copy.start()
        stores.append(copy)
    for copy in sent:
        copy.wait_send()
    for copy in stores:
        copy.wait()


def fast_device(
    pools, prompt_states, stretch_slot, cache_length, cache_keys, cache_values, step_states,
    query_weight, key_weight, value_weight,
):
    count = lax.axis_size("tp")
    pool = lax.axis_index("pool")
    real_rows = prompt_states.shape[0]
    local = cache_length.shape[0]
    block = STEPS * local
    half = block // 2
    padded = real_rows + half
    depth = prompt_states.shape[1]
    width = query_weight.shape[1]
    widths = (width, key_weight.shape[1], value_weight.shape[1])
    slots = jnp.pad(
        stretch_slot.reshape(pools * count, real_rows),
        ((0, 0), (0, padded - real_rows)),
        constant_values=-1,
    ).reshape(pools, count * padded)
    freq = frequencies(HEAD // 2)
    freq = jnp.concatenate([freq, freq])[None, :]
    inside = pl.BlockSpec(memory_space=pltpu.VMEM)
    anywhere = pl.BlockSpec(memory_space=pl.ANY)
    heads = width // HEAD
    kinds = 1 + 4 * (count // 2 - 1)
    bf16, f32 = jnp.bfloat16, jnp.float32
    wave = pltpu.SemaphoreType.DMA((2, kinds, CHUNKS))
    return pl.pallas_call(
        functools.partial(whole_kernel, pools, count, real_rows, 1.0 / math.sqrt(HEAD)),
        out_shape=[
            jax.ShapeDtypeStruct((count * real_rows, width), bf16),
            jax.ShapeDtypeStruct((STEPS, local, count * width), bf16),
        ],
        in_specs=[inside] * 2
        + [anywhere] * 3
        + [inside] * 2
        + [pl.BlockSpec(memory_space=pltpu.SMEM)]
        + [anywhere] * 2,
        out_specs=[anywhere] * 2,
        scratch_shapes=[pltpu.VMEM((count * padded, w), bf16) for w in widths]
        + [pltpu.VMEM((count * block, w), bf16) for w in widths]
        + [
            pltpu.VMEM((count, padded, depth), bf16),
            pltpu.VMEM((count, 4 * half, depth // 4), bf16),
        ]
        + [pltpu.VMEM((depth, w), bf16) for w in widths]
        + [pltpu.VMEM((count * (padded + half), w), f32) for w in widths]
        + [
            pltpu.VMEM((count * real_rows, width), bf16),
            pltpu.VMEM((STEPS, local, count * width), bf16),
            pltpu.VMEM((2, count * padded, HEAD), f32),
            pltpu.VMEM((2, count * block, HEAD), f32),
            pltpu.VMEM((2, block, HEAD), f32),
            pltpu.VMEM((pools, count * padded, 2 * HEAD), bf16),
            pltpu.VMEM((count, block, width + 2 * HEAD), bf16),
            pltpu.VMEM((count, block, width + 2 * HEAD), bf16),
            pltpu.VMEM(cache_keys.shape, bf16),
            pltpu.VMEM(cache_values.shape, bf16),
            pltpu.SemaphoreType.DMA((3, CHUNKS)),
            wave,
            wave,
            pltpu.SemaphoreType.DMA((2,)),
            pltpu.SemaphoreType.DMA((heads + count,)),
            pltpu.SemaphoreType.DMA((pools - 1,)),
            pltpu.SemaphoreType.DMA((pools - 1,)),
            pltpu.SemaphoreType.DMA((count - 1,)),
            pltpu.SemaphoreType.DMA((count - 1,)),
        ],
        compiler_params=pltpu.CompilerParams(
            collective_id=0, has_side_effects=True, vmem_limit_bytes=VMEM_LIMIT
        ),
    )(
        prompt_states, step_states, query_weight, key_weight, value_weight,
        slots, freq, cache_length, cache_keys, cache_values,
    )


def per_device(pools, *args):
    count = lax.axis_size("tp")
    extra = args[2].shape[0] * STEPS // 2
    if count == KV_HEADS and args[7].shape[1] == HEAD and extra == 4 and (args[0].shape[0] + extra) % 16 == 0:
        return fast_device(pools, *args)
    return on_device(*args)


def solution(mesh):
    in_specs = (
        P(("pool", "tp"), None),
        P(),
        P(("pool", "tp")),
        P(("pool", "tp"), None, None),
        P(("pool", "tp"), None, None),
        P(None, ("pool", "tp"), None),
        P(None, "tp"),
        P(None, "tp"),
        P(None, "tp"),
    )
    out_specs = (P("pool", "tp"), P(None, ("pool", "tp"), None))
    return jax.shard_map(
        functools.partial(per_device, mesh.shape["pool"]), mesh=mesh, in_specs=in_specs, out_specs=out_specs, check_vma=False
    )
```
